32 devices in a mesh: tiles: 2 (over y), row: 8 (over z, x), col: 2 (over core).
Axes of the slice: x: 2, y: 2, z: 4, core: 2. Of those that a mesh axis runs over, the one named last changes fastest.
Arguments:
- layers: float32 [8, 4096, 4096], P('tiles', 'row', 'col'), parts along dimension 0, may hold values from -6 to 6
- unmixing: bfloat16 [4, 4, 4, 2048, 4096], P('tiles', None, None, ('row', 'col')), parts along dimension 0, may hold values from -2 to 2
Outputs:
- components: float32 [8, 4096, 4096], P('tiles', 'row', 'col'), parts along dimension 0
The draws below stay inside these ranges and needn't reach their ends.
There are 2 independent parts, one for each index of `tiles`. The reference program is written for one: setup_inputs(seed, part) draws one part's arguments, and reference() takes and returns one part's arrays. A program takes and returns all parts, laid end to end along the dimension named above; each array names one. Nothing has to cross between parts.
All inputs are finite; a program needn't handle non-finite values.
Results may differ from the reference program's by a relative error of at most 0.0003.
Values sent between devices are 32-bit elements; how exact they have to be, the bound alone decides.
No kernel may reach another device: no remote copies, remote signals or barrier semaphores. Data moves between devices by JAX's collectives and lax.ppermute only.
A program may use at most 320 MiB of HBM per device.

```python
import jax
import jax.numpy as jnp

N1 = 4096
N2 = 4096
HALF = 2048


def shard_levels(stream_key, dims, shards, smallest, high):
    def one(position, parts):
        steps = jax.random.uniform(jax.random.fold_in(jax.random.fold_in(stream_key, 6), position), (parts,), jnp.float32, smallest / len(shards), high / len(shards))
        return jnp.repeat(jnp.exp(steps), dims[position] // parts).reshape((-1,) + (1,) * (len(dims) - position - 1))

    loudness = one(*shards[0])
    for cut in shards[1:]:
        loudness = loudness * one(*cut)
    return loudness


def scatter_about(key, extent, width, reach, pieces=(), dtype=jnp.bfloat16):
    values = width * jax.random.normal(key, extent, jnp.float32)
    if pieces:
        values = values * shard_levels(key, extent, pieces, -0.22, 0.18)
    return jnp.clip(values, -reach, reach).astype(dtype)


def setup_inputs(seed: int = 0, part: int = 0) -> dict:
    splits = jax.random.split(jax.random.key(seed), 3)
    part_splits = jax.random.split(jax.random.fold_in(splits[2], part), 3)
    layers = scatter_about(part_splits[0], (4, N1, N2), 1.0, 6.0, ((1, 8), (2, 2)), jnp.float32)
    unmixing = scatter_about(part_splits[1], (2, 4, 4, HALF, N1), 0.35, 2.0, ((3, 16),))
    return {"layers": layers, "unmixing": unmixing}


def reference(layers, unmixing):
    half = N2 // 2
    spectra = jnp.fft.fft(jnp.fft.rfft(layers, axis=2)[:, :, :half], axis=1)
    spectra = jnp.transpose(spectra, (0, 2, 1))
    wave_real = jnp.real(spectra)
    wave_imag = jnp.imag(spectra)
    results = []
    for index in range(4):
        weight_real = unmixing[0, index].astype(jnp.float32)
        weight_imag = unmixing[1, index].astype(jnp.float32)
        mixed_real = jnp.sum(weight_real * wave_real - weight_imag * wave_imag, axis=0)
        mixed_imag = jnp.sum(weight_real * wave_imag + weight_imag * wave_real, axis=0)
        mixed = jnp.transpose(mixed_real + 1j * mixed_imag)
        padded = jnp.concatenate([mixed, jnp.zeros_like(mixed)], axis=1)
        field = 2.0 * jnp.real(jnp.fft.ifft2(padded))
        results.append(field.astype(jnp.float32))
    return jnp.stack(results, axis=0)
```

```python
import math

import jax
import jax.numpy as jnp
import ml_dtypes
import numpy as np
from jax import lax
from jax.experimental import pallas as pl
from jax.experimental.pallas import tpu as pltpu
from jax.sharding import PartitionSpec as P

RADIX = 16


def split_table(table):
    high = table.astype(ml_dtypes.bfloat16)
    low = (table - high.astype(np.float64)).astype(ml_dtypes.bfloat16)
    return np.stack([high, low])


def twiddle_table(count, width, length, sign):
    turns = np.outer(np.arange(count), np.arange(width)) % length
    phase = turns * (sign * 2.0 * math.pi / length)
    pair = np.stack([np.cos(phase), np.sin(phase)], axis=1)
    return np.ascontiguousarray(
        np.broadcast_to(pair[:, :, None, :], (count, 2, 8, width))
    ).astype(np.float32)


def line_table(out_len, width, sign):
    turns = np.outer(np.arange(out_len), np.arange(width)) % width
    phase = turns * (sign * 2.0 * math.pi / width)
    return split_table(np.concatenate([np.cos(phase), np.sin(phase)], axis=0))


def real_table(out_len, width, scale):
    turns = np.outer(np.arange(out_len), np.arange(width)) % width
    phase = turns * (2.0 * math.pi / width)
    return split_table(scale * np.concatenate([np.cos(phase), -np.sin(phase)], axis=1))


def turn(value, numerator, denominator):
    real, imag = value
    numerator %= denominator
    eighths = 8 * numerator / denominator
    if eighths == 0:
        return (real, imag)
    if eighths == 2:
        return (-imag, real)
    if eighths == 4:
        return (-real, -imag)
    if eighths == 6:
        return (imag, -real)
    cos = math.cos(2.0 * math.pi * numerator / denominator)
    sin = math.sin(2.0 * math.pi * numerator / denominator)
    if eighths in (1, 3, 5, 7):
        half = math.sqrt(0.5)
        scaled_sum = (real + imag) * half
        scaled_gap = (real - imag) * half
        if eighths == 1:
            return (scaled_gap, scaled_sum)
        if eighths == 3:
            return (-scaled_sum, scaled_gap)
        if eighths == 5:
            return (-scaled_gap, -scaled_sum)
        return (scaled_sum, -scaled_gap)
    return (real * cos - imag * sin, real * sin + imag * cos)


def add(left, right):
    return (left[0] + right[0], left[1] + right[1])


def gap(left, right):
    return (left[0] - right[0], left[1] - right[1])


def small_fourier(values, sign):
    count = len(values)
    if count == 1:
        return values
    even = small_fourier(values[0::2], sign)
    odd = small_fourier(values[1::2], sign)
    odd = [turn(value, sign * index, count) for index, value in enumerate(odd)]
    return [add(e, o) for e, o in zip(even, odd)] + [gap(e, o) for e, o in zip(even, odd)]


def small_real_fourier(values, sign):
    count = len(values)
    if count == 2:
        zero = jnp.zeros_like(values[0])
        return [(values[0] + values[1], zero), (values[0] - values[1], zero)]
    even = small_real_fourier(values[0::2], sign)
    odd = small_real_fourier(values[1::2], sign)
    result = [None] * count
    for index in range(count // 4 + 1):
        turned = turn(odd[index], sign * index, count)
        upper = add(even[index], turned)
        lower = gap(even[index], turned)
        result[index] = upper
        result[count // 2 - index] = (lower[0], -lower[1])
    for index in range(1, count // 2):
        result[count - index] = (result[index][0], -result[index][1])
    return result


def twist(value, table_ref, index, lanes):
    if index == 0:
        return value
    cos = table_ref[index, 0, :, lanes]
    sin = table_ref[index, 1, :, lanes]
    return (value[0] * cos - value[1] * sin, value[0] * sin + value[1] * cos)


def dot_rows(table, values):
    return lax.dot_general(
        table, values, (((1,), (1,)), ((), ())), preferred_element_type=jnp.float32
    )


def matmul_split(table_ref, values):
    high = values.astype(jnp.bfloat16)
    low = (values - high.astype(jnp.float32)).astype(jnp.bfloat16)
    return (
        dot_rows(table_ref[0], high)
        + dot_rows(table_ref[0], low)
        + dot_rows(table_ref[1], high)
    )


def combine(products, out_len, rows):
    cos_part = products[:out_len]
    sin_part = products[out_len:]
    real = cos_part[:, :rows] - sin_part[:, rows:]
    imag = cos_part[:, rows:] + sin_part[:, :rows]
    return real, imag


def row_forward_kernel(core_ref, own_ref, other_ref, twist_ref, table_ref, out_ref, part_ref):
    rows = own_ref.shape[1]
    width = part_ref.shape[2]
    per_half = RADIX // 2

    def small(step, _):
        row = pl.multiple_of(step * 8, 8)
        for lane in range(width // 128):
            lanes = pl.ds(lane * 128, 128)
            values = [
                half_ref[0, pl.ds(row, 8), pl.ds(index * width + lane * 128, 128)]
                for half_ref in (own_ref, other_ref)
                for index in range(per_half)
            ]
            for index, value in enumerate(small_real_fourier(values, -1)):
                real, imag = twist(value, twist_ref, index, lanes)
                part_ref[index, pl.ds(row, 8), lanes] = real
                part_ref[index, pl.ds(rows + row, 8), lanes] = imag
        return 0

    lax.fori_loop(0, rows // 8, small, 0)
    blocks, _, _, per_block, _ = out_ref.shape
    out_len = blocks * per_block // RADIX
    piece = per_block // RADIX

    def line(index, _):
        real, imag = combine(matmul_split(table_ref, part_ref[index]), out_len, rows)
        for block in range(blocks):
            place = pl.ds(index, piece, stride=RADIX)
            out_ref[block, 0, 0, place, :] = real[block * piece : (block + 1) * piece]
            out_ref[block, 0, 1, place, :] = imag[block * piece : (block + 1) * piece]
        return 0

    lax.fori_loop(0, RADIX, line, 0)


def complex_lines(read, rows, width, sign, twist_ref, part_ref):
    def small(step, _):
        row = pl.multiple_of(step * 8, 8)
        for lane in range(width // 128):
            lanes = pl.ds(lane * 128, 128)
            values = [
                (read(index, 0, pl.ds(row, 8), lanes), read(index, 1, pl.ds(row, 8), lanes))
                for index in range(RADIX)
            ]
            for index, value in enumerate(small_fourier(values, sign)):
                real, imag = twist(value, twist_ref, index, lanes)
                part_ref[index, pl.ds(row, 8), lanes] = real
                part_ref[index, pl.ds(rows + row, 8), lanes] = imag
        return 0

    lax.fori_loop(0, rows // 8, small, 0)


def column_forward_kernel(x_ref, twist_ref, table_ref, out_ref, part_ref, order_ref):
    rows = x_ref.shape[3]
    width = x_ref.shape[4]

    def read(index, part, row, lanes):
        return x_ref[index, 0, part, row, lanes]

    complex_lines(read, rows, width, -1, twist_ref, part_ref)

    def line(index, _):
        real, imag = combine(matmul_split(table_ref, part_ref[index]), width, rows)
        order_ref[0, pl.ds(index, width, stride=RADIX), :] = real
        order_ref[1, pl.ds(index, width, stride=RADIX), :] = imag
        return 0

    lax.fori_loop(0, RADIX, line, 0)

    def flip(index, _):
        start = pl.multiple_of(index * width, width)
        for part in range(2):
            out_ref[0, part, :, pl.ds(start, width)] = order_ref[part, pl.ds(start, width), :].T
        return 0

    lax.fori_loop(0, RADIX, flip, 0)


def mix_rows(waves, unmix_ref, row, real, imag):
    for layer, wave in enumerate(waves):
        weight_real = unmix_ref[0, 0, layer, pl.ds(row, 16), :].astype(jnp.float32)
        weight_imag = unmix_ref[1, 0, layer, pl.ds(row, 16), :].astype(jnp.float32)
        wave_real = wave[0, 0, pl.ds(row, 16), :]
        wave_imag = wave[0, 1, pl.ds(row, 16), :]
        term_real = weight_real * wave_real - weight_imag * wave_imag
        term_imag = weight_real * wave_imag + weight_imag * wave_real
        real = term_real if real is None else real + term_real
        imag = term_imag if imag is None else imag + term_imag
    return real, imag


def partial_mix_kernel(w0_ref, w1_ref, w2_ref, unmix_ref, out_ref):
    def mix(block, _):
        row = pl.multiple_of(block * 16, 16)
        real, imag = mix_rows((w0_ref, w1_ref, w2_ref), unmix_ref, row, None, None)
        out_ref[0, 0, pl.ds(row, 16), :] = real
        out_ref[0, 1, pl.ds(row, 16), :] = imag
        return 0

    lax.fori_loop(0, out_ref.shape[2] // 16, mix, 0)


def column_inverse_kernel(
    sum_ref, wave_ref, unmix_ref, twist_ref, table_ref, out_ref, mixed_ref, part_ref
):
    step = pl.program_id(1)
    rows = mixed_ref.shape[2]
    width = mixed_ref.shape[3]

    def mix(block, _):
        row = pl.multiple_of(block * 16, 16)
        real, imag = mix_rows(
            (wave_ref,),
            unmix_ref,
            row,
            sum_ref[0, 0, pl.ds(row, 16), :],
            sum_ref[0, 1, pl.ds(row, 16), :],
        )
        mixed_ref[step, 0, pl.ds(row, 16), :] = real
        mixed_ref[step, 1, pl.ds(row, 16), :] = imag
        return 0

    lax.fori_loop(0, rows // 16, mix, 0)

    @pl.when(step == RADIX - 1)
    def _():
        def read(index, part, row, lanes):
            return mixed_ref[index, part, row, lanes]

        complex_lines(read, rows, width, 1, twist_ref, part_ref)
        blocks, _, _, per_block, _ = out_ref.shape
        piece = per_block // RADIX

        def line(index, _):
            real, imag = combine(matmul_split(table_ref, part_ref[index]), width, rows)
            for block in range(blocks):
                place = pl.ds(index, piece, stride=RADIX)
                out_ref[block, 0, 0, place, :] = real[block * piece : (block + 1) * piece]
                out_ref[block, 0, 1, place, :] = imag[block * piece : (block + 1) * piece]
            return 0

        lax.fori_loop(0, RADIX, line, 0)


def row_inverse_kernel(core_ref, x_ref, twist_ref, table_ref, *refs):
    out_ref, sent_ref, part_ref, order_ref = refs[-4:]
    rows = x_ref.shape[3]
    width = x_ref.shape[4]
    count = 2 * RADIX
    lanes = pl.ds(0, width)

    def small(step, _):
        row = pl.multiple_of(step * 8, 8)
        for odd in range(2):
            values = [
                (x_ref[index, 0, 0, pl.ds(row, 8), :], x_ref[index, 0, 1, pl.ds(row, 8), :])
                for index in range(RADIX)
            ]
            if odd:
                values = [turn(value, index, count) for index, value in enumerate(values)]
            for index, value in enumerate(small_fourier(values, 1)):
                real, imag = twist(value, twist_ref, 2 * index + odd, lanes)
                part_ref[2 * index + odd, pl.ds(row, 8), pl.ds(0, width)] = real
                part_ref[2 * index + odd, pl.ds(row, 8), pl.ds(width, width)] = imag
        return 0

    lax.fori_loop(0, rows // 8, small, 0)
    out_len = table_ref.shape[1]

    def line(index, _):
        order_ref[pl.ds(index, out_len, stride=count), :] = matmul_split(table_ref, part_ref[index])
        return 0

    lax.fori_loop(0, count, line, 0)
    half_len = sent_ref.shape[1]
    chunk = 256
    own = core_ref[0] * half_len
    other = half_len - own

    def flip(index, _):
        start = pl.multiple_of(index * chunk, chunk)
        own_start = pl.multiple_of(own + start, chunk)
        other_start = pl.multiple_of(other + start, chunk)
        sent_ref[:, pl.ds(start, chunk)] = order_ref[pl.ds(other_start, chunk), :].T
        out_ref[0, :, pl.ds(start, chunk)] = order_ref[pl.ds(own_start, chunk), :].T
        return 0

    lax.fori_loop(0, half_len // chunk, flip, 0)


def whole(array):
    return pl.BlockSpec(array.shape, lambda *_: (0,) * array.ndim)


VMEM_LIMIT = 56 * 1024 * 1024
ROW_TILE = 128


def params(rank):
    return pltpu.CompilerParams(
        dimension_semantics=("arbitrary",) * rank, vmem_limit_bytes=VMEM_LIMIT
    )


def row_forward(layers, other, core, first, blocks, per_block):
    count, rows, half_len = other.shape
    length = 2 * half_len
    width = length // RADIX
    tiles = rows // ROW_TILE
    signs = jnp.where(jnp.arange(RADIX) % 2 == 1, 1.0 - 2.0 * core[0].astype(jnp.float32), 1.0)
    twists = jnp.asarray(twiddle_table(RADIX, width, length, -1)) * signs[:, None, None, None]
    table = jnp.asarray(line_table(blocks * per_block // RADIX, width, -1))
    return pl.pallas_call(
        row_forward_kernel,
        grid_spec=pltpu.PrefetchScalarGridSpec(
            num_scalar_prefetch=1,
            grid=(count, tiles),
            in_specs=[
                pl.BlockSpec(
                    (1, ROW_TILE, half_len), lambda m, i, c: (first + m, c[0] * tiles + i, 0)
                ),
                pl.BlockSpec((1, ROW_TILE, half_len), lambda m, i, c: (m, i, 0)),
                whole(twists),
                whole(table),
            ],
            out_specs=pl.BlockSpec(
                (blocks, 1, 2, per_block, ROW_TILE), lambda m, i, c: (0, m, 0, 0, i)
            ),
            scratch_shapes=[pltpu.VMEM((RADIX, 2 * ROW_TILE, width), jnp.float32)],
        ),
        out_shape=jax.ShapeDtypeStruct((blocks, count, 2, per_block, rows), jnp.float32),
        compiler_params=params(2),
        name="row_forward",
    )(core, layers, other, twists, table)


def column_forward(x):
    blocks, count, _, rows, width = x.shape
    length = RADIX * width
    twists = jnp.asarray(twiddle_table(RADIX, width, length, -1))
    table = jnp.asarray(line_table(width, width, -1))
    return pl.pallas_call(
        column_forward_kernel,
        grid=(count,),
        in_specs=[
            pl.BlockSpec((blocks, 1, 2, rows, width), lambda m: (0, m, 0, 0, 0)),
            whole(twists),
            whole(table),
        ],
        out_specs=pl.BlockSpec((1, 2, rows, length), lambda m: (m, 0, 0, 0)),
        out_shape=jax.ShapeDtypeStruct((count, 2, rows, length), jnp.float32),
        scratch_shapes=[
            pltpu.VMEM((RADIX, 2 * rows, width), jnp.float32),
            pltpu.VMEM((2, length, rows), jnp.float32),
        ],
        compiler_params=params(1),
        name="column_forward",
    )(x, twists, table)


def partial_mix(waves, unmixing):
    components = unmixing.shape[1]
    _, _, rows, length = waves[0][0].shape
    width = length // RADIX

    def wave_spec(place):
        return pl.BlockSpec((1, 2, rows, width), lambda i, j: (place, 0, 0, i))

    return pl.pallas_call(
        partial_mix_kernel,
        grid=(RADIX, components),
        in_specs=[wave_spec(place) for _, place in waves]
        + [pl.BlockSpec((2, 1, len(waves), rows, width), lambda i, j: (0, j, 0, 0, i))],
        out_specs=pl.BlockSpec((1, 2, rows, width), lambda i, j: (j, 0, 0, i)),
        out_shape=jax.ShapeDtypeStruct((components, 2, rows, length), jnp.float32),
        compiler_params=params(2),
        name="partial_mix",
    )(*[wave for wave, _ in waves], unmixing)


def column_inverse(sums, wave, place, layer, unmixing, first, count, blocks):
    _, _, rows, length = sums.shape
    width = length // RADIX
    per_block = length // blocks
    twists = jnp.asarray(twiddle_table(RADIX, width, length, 1))
    table = jnp.asarray(line_table(width, width, 1))
    return pl.pallas_call(
        column_inverse_kernel,
        grid=(count, RADIX),
        in_specs=[
            pl.BlockSpec((1, 2, rows, width), lambda j, i: (first + j, 0, 0, i)),
            pl.BlockSpec((1, 2, rows, width), lambda j, i: (place, 0, 0, i)),
            pl.BlockSpec((2, 1, 1, rows, width), lambda j, i: (0, first + j, layer, 0, i)),
            whole(twists),
            whole(table),
        ],
        out_specs=pl.BlockSpec((blocks, 1, 2, per_block, rows), lambda j, i: (0, j, 0, 0, 0)),
        out_shape=jax.ShapeDtypeStruct((blocks, count, 2, per_block, rows), jnp.float32),
        scratch_shapes=[
            pltpu.VMEM((RADIX, 2, rows, width), jnp.float32),
            pltpu.VMEM((RADIX, 2 * rows, width), jnp.float32),
        ],
        compiler_params=params(2),
        name="column_inverse",
    )(sums, wave, unmixing, twists, table)


def row_inverse(x, place, component, shape, fields, core, scale):
    blocks, _, _, rows, width = x.shape
    half_len = shape[2]
    length = 2 * half_len
    count = 2 * RADIX
    tiles = rows // ROW_TILE
    twists = jnp.asarray(twiddle_table(count, width, length, 1))
    table = jnp.asarray(real_table(length // count, width, scale))
    held = [] if fields is None else [fields]
    return pl.pallas_call(
        row_inverse_kernel,
        grid_spec=pltpu.PrefetchScalarGridSpec(
            num_scalar_prefetch=1,
            grid=(tiles,),
            in_specs=[
                pl.BlockSpec((blocks, 1, 2, ROW_TILE, width), lambda i, c: (0, place, 0, i, 0)),
                whole(twists),
                whole(table),
            ]
            + [pl.BlockSpec(memory_space=pl.ANY)] * len(held),
            out_specs=[
                pl.BlockSpec(
                    (1, ROW_TILE, half_len), lambda i, c: (component, c[0] * tiles + i, 0)
                ),
                pl.BlockSpec((ROW_TILE, half_len), lambda i, c: (i, 0)),
            ],
            scratch_shapes=[
                pltpu.VMEM((count, ROW_TILE, 2 * width), jnp.float32),
                pltpu.VMEM((length, ROW_TILE), jnp.float32),
            ],
        ),
        out_shape=[
            jax.ShapeDtypeStruct(shape, jnp.float32),
            jax.ShapeDtypeStruct((rows, half_len), jnp.float32),
        ],
        input_output_aliases={4: 0} if held else {},
        compiler_params=params(1),
        name="row_inverse",
    )(core, x, twists, table, *held)


def phase_pair(first_len, second_len, period, sign):
    first = lax.broadcasted_iota(jnp.int32, (first_len, second_len), 0)
    second = lax.broadcasted_iota(jnp.int32, (first_len, second_len), 1)
    turns = (first * second % period).astype(jnp.float32)
    phase = turns * (sign * 2.0 * math.pi / period)
    return (jnp.cos(phase), jnp.sin(phase))


def contract_first(values, table):
    return jnp.einsum("...qp,qk->...pk", values, table, precision=lax.Precision.HIGHEST)


def contract_second(values, table):
    return jnp.einsum("...pk,pj->...jk", values, table, precision=lax.Precision.HIGHEST)


def fourier(real_in, imag_in, length, sign, in_len, out_len, real_only):
    inner_len = min(length, 128)
    outer_len = length // inner_len
    rows_in = in_len // outer_len
    rows_out = out_len // inner_len
    leading = real_in.shape[:-1]
    first_cos, first_sin = phase_pair(rows_in, inner_len, inner_len, sign)
    first_table = jnp.concatenate([first_cos, first_sin], axis=1)
    both = contract_first(real_in.reshape(leading + (rows_in, outer_len)), first_table)
    part_real = both[..., :inner_len]
    part_imag = both[..., inner_len:]
    if imag_in is not None:
        other = contract_first(imag_in.reshape(leading + (rows_in, outer_len)), first_table)
        part_real = part_real - other[..., inner_len:]
        part_imag = part_imag + other[..., :inner_len]
    twist_cos, twist_sin = phase_pair(outer_len, inner_len, length, sign)
    turned_real = part_real * twist_cos - part_imag * twist_sin
    turned_imag = part_real * twist_sin + part_imag * twist_cos
    stacked = jnp.concatenate([turned_real, turned_imag], axis=-2)
    second_cos, second_sin = phase_pair(outer_len, rows_out, outer_len, sign)
    table_real = jnp.concatenate([second_cos, -second_sin], axis=0)
    if real_only:
        result_real = contract_second(stacked, table_real)
        return result_real.reshape(leading + (out_len,))
    table_imag = jnp.concatenate([second_sin, second_cos], axis=0)
    combined = contract_second(stacked, jnp.concatenate([table_real, table_imag], axis=1))
    result_real = combined[..., :rows_out, :].reshape(leading + (out_len,))
    result_imag = combined[..., rows_out:, :].reshape(leading + (out_len,))
    return (result_real, result_imag)


def reorder_blocks(values, row_count, col_count):
    leading = values.shape[0]
    block = values.shape[1] // (row_count * col_count)
    width = values.shape[2]
    split = values.reshape(leading, col_count, row_count, block, width)
    return jnp.transpose(split, (0, 4, 2, 1, 3)).reshape(
        leading, width, row_count * col_count * block
    )


def general_shards(layers, unmixing):
    row_count = lax.axis_size("row")
    col_count = lax.axis_size("col")
    rows_len = layers.shape[1] * row_count
    cols_len = layers.shape[2] * col_count
    spec_real, spec_imag = fourier(
        lax.all_to_all(layers, "col", split_axis=1, concat_axis=2, tiled=True),
        None,
        cols_len,
        -1.0,
        cols_len,
        cols_len // 2,
        False,
    )
    moved_real, moved_imag = (
        lax.all_to_all(
            lax.all_to_all(spec_real, "row", split_axis=2, concat_axis=1, tiled=True),
            "col",
            split_axis=2,
            concat_axis=1,
            tiled=True,
        ),
        lax.all_to_all(
            lax.all_to_all(spec_imag, "row", split_axis=2, concat_axis=1, tiled=True),
            "col",
            split_axis=2,
            concat_axis=1,
            tiled=True,
        ),
    )
    line_real = reorder_blocks(moved_real, row_count, col_count)
    line_imag = reorder_blocks(moved_imag, row_count, col_count)
    wave_real, wave_imag = fourier(line_real, line_imag, rows_len, -1.0, rows_len, rows_len, False)
    mixed_real = None
    mixed_imag = None
    for layer_index in range(4):
        weight_real = unmixing[0, :, layer_index].astype(jnp.float32)
        weight_imag = unmixing[1, :, layer_index].astype(jnp.float32)
        layer_real = wave_real[layer_index][None]
        layer_imag = wave_imag[layer_index][None]
        term_real = weight_real * layer_real - weight_imag * layer_imag
        term_imag = weight_real * layer_imag + weight_imag * layer_real
        if mixed_real is None:
            mixed_real = term_real
            mixed_imag = term_imag
        else:
            mixed_real = mixed_real + term_real
            mixed_imag = mixed_imag + term_imag
    back_real, back_imag = fourier(mixed_real, mixed_imag, rows_len, 1.0, rows_len, rows_len, False)
    scale = 2.0 / (rows_len * cols_len)
    sent_real, sent_imag = (
        lax.all_to_all(
            lax.all_to_all(back_real, "row", split_axis=2, concat_axis=1, tiled=True),
            "col",
            split_axis=2,
            concat_axis=1,
            tiled=True,
        ),
        lax.all_to_all(
            lax.all_to_all(back_imag, "row", split_axis=2, concat_axis=1, tiled=True),
            "col",
            split_axis=2,
            concat_axis=1,
            tiled=True,
        ),
    )
    grid_real = reorder_blocks(sent_real, row_count, col_count)
    grid_imag = reorder_blocks(sent_imag, row_count, col_count)
    fields = fourier(grid_real, grid_imag, cols_len, 1.0, cols_len // 2, cols_len, True)
    fields = fields * scale
    return lax.all_to_all(fields, "col", split_axis=2, concat_axis=1, tiled=True)


def swap_cores(values):
    return lax.ppermute(values, "col", [(0, 1), (1, 0)])


def exchange(values):
    return lax.all_to_all(values, ("row", "col"), split_axis=0, concat_axis=0, tiled=True)


def layer_shards(layers, unmixing):
    row_count = lax.axis_size("row")
    col_count = lax.axis_size("col")
    blocks = row_count * col_count
    _, block_rows, half_len = layers.shape
    rows = block_rows // col_count
    per_block = unmixing.shape[3]
    core = lax.axis_index("col").astype(jnp.int32).reshape(1)
    own_row = core[0] * rows
    other_row = rows - own_row
    groups = ((0, 1), (1, 2), (3, 1))

    source = layers
    moved = None
    arrived = []
    for first, count in groups:
        given = lax.dynamic_slice(source, (first, other_row, 0), (count, rows, half_len))
        spectra = row_forward(layers, swap_cores(given), core, first, blocks, per_block)
        source, spectra = lax.optimization_barrier((source, spectra))
        if moved is not None:
            spectra, moved = lax.optimization_barrier((spectra, moved))
        moved = exchange(spectra)
        arrived.append(moved)
    waves = []
    for (_, count), moved in zip(groups, arrived):
        group = column_forward(moved)
        waves += [(group, place) for place in range(count)]
    sums = partial_mix(waves[:3], unmixing)
    scale = 2.0 / (block_rows * row_count * half_len * col_count)
    fields = None
    for first, count in groups:
        back = column_inverse(sums, *waves[3], 3, unmixing, first, count, blocks)
        if first > 0:
            back, sent = lax.optimization_barrier((back, sent))
        sent = exchange(back)
        for place in range(count):
            fields, given = row_inverse(
                sent, place, first + place, layers.shape, fields, core, scale
            )
            taken = swap_cores(given)[None]
            fields = lax.dynamic_update_slice(fields, taken, (first + place, other_row, 0))
    return fields


def shards(layers, unmixing):
    col_count = lax.axis_size("col")
    blocks = lax.axis_size("row") * col_count
    shape = (blocks, col_count) + layers.shape + unmixing.shape[1:]
    if shape == (RADIX, 2, 4, 512, 2048, 4, 4, 128, 4096):
        return layer_shards(layers, unmixing)
    return general_shards(layers, unmixing)


def solution(mesh):
    in_specs = (P("tiles", "row", "col"), P("tiles", None, None, ("row", "col"), None))
    out_specs = P("tiles", "row", "col")
    return jax.shard_map(shards, mesh=mesh, in_specs=in_specs, out_specs=out_specs, check_vma=False)
```

```python
import functools
import math

import jax
import jax.numpy as jnp
import ml_dtypes
import numpy as np
from jax import lax
from jax.experimental import pallas as pl
from jax.experimental.pallas import tpu as pltpu
from jax.sharding import PartitionSpec as P

RADIX = 16
PACKED = 64


def split_table(table):
    high = table.astype(ml_dtypes.bfloat16)
    low = (table - high.astype(np.float64)).astype(ml_dtypes.bfloat16)
    return np.stack([high, low])


def twiddle_table(count, width, length, sign):
    turns = np.outer(np.arange(count), np.arange(width)) % length
    phase = turns * (sign * 2.0 * math.pi / length)
    pair = np.stack([np.cos(phase), np.sin(phase)], axis=1)
    return np.ascontiguousarray(
        np.broadcast_to(pair[:, :, None, :], (count, 2, 8, width))
    ).astype(np.float32)


def line_table(out_len, width, sign):
    turns = np.outer(np.arange(out_len), np.arange(width)) % width
    phase = turns * (sign * 2.0 * math.pi / width)
    return split_table(np.concatenate([np.cos(phase), np.sin(phase)], axis=0))


def real_table(out_len, width, scale):
    turns = np.outer(np.arange(out_len), np.arange(width)) % width
    phase = turns * (2.0 * math.pi / width)
    return split_table(scale * np.concatenate([np.cos(phase), -np.sin(phase)], axis=1))


def turn(value, numerator, denominator):
    real, imag = value
    numerator %= denominator
    eighths = 8 * numerator / denominator
    if eighths == 0:
        return (real, imag)
    if eighths == 2:
        return (-imag, real)
    if eighths == 4:
        return (-real, -imag)
    if eighths == 6:
        return (imag, -real)
    cos = math.cos(2.0 * math.pi * numerator / denominator)
    sin = math.sin(2.0 * math.pi * numerator / denominator)
    if eighths in (1, 3, 5, 7):
        half = math.sqrt(0.5)
        scaled_sum = (real + imag) * half
        scaled_gap = (real - imag) * half
        if eighths == 1:
            return (scaled_gap, scaled_sum)
        if eighths == 3:
            return (-scaled_sum, scaled_gap)
        if eighths == 5:
            return (-scaled_gap, -scaled_sum)
        return (scaled_sum, -scaled_gap)
    return (real * cos - imag * sin, real * sin + imag * cos)


def add(left, right):
    return (left[0] + right[0], left[1] + right[1])


def gap(left, right):
    return (left[0] - right[0], left[1] - right[1])


def small_fourier(values, sign):
    count = len(values)
    if count == 1:
        return values
    even = small_fourier(values[0::2], sign)
    odd = small_fourier(values[1::2], sign)
    odd = [turn(value, sign * index, count) for index, value in enumerate(odd)]
    return [add(e, o) for e, o in zip(even, odd)] + [gap(e, o) for e, o in zip(even, odd)]


def small_real_fourier(values, sign):
    count = len(values)
    if count == 2:
        zero = jnp.zeros_like(values[0])
        return [(values[0] + values[1], zero), (values[0] - values[1], zero)]
    even = small_real_fourier(values[0::2], sign)
    odd = small_real_fourier(values[1::2], sign)
    result = [None] * count
    for index in range(count // 4 + 1):
        turned = turn(odd[index], sign * index, count)
        upper = add(even[index], turned)
        lower = gap(even[index], turned)
        result[index] = upper
        result[count // 2 - index] = (lower[0], -lower[1])
    for index in range(1, count // 2):
        result[count - index] = (result[index][0], -result[index][1])
    return result


def twist(value, table_ref, index, lanes):
    if index == 0:
        return value
    cos = table_ref[index, 0, :, lanes]
    sin = table_ref[index, 1, :, lanes]
    return (value[0] * cos - value[1] * sin, value[0] * sin + value[1] * cos)


def dot_rows(table, values):
    return lax.dot_general(
        table, values, (((1,), (1,)), ((), ())), preferred_element_type=jnp.float32
    )


def matmul_split(table_ref, values):
    high = values.astype(jnp.bfloat16)
    low = (values - high.astype(jnp.float32)).astype(jnp.bfloat16)
    return (
        dot_rows(table_ref[0], high)
        + dot_rows(table_ref[0], low)
        + dot_rows(table_ref[1], high)
    )


def combine(products, out_len, rows):
    cos_part = products[:out_len]
    sin_part = products[out_len:]
    real = cos_part[:, :rows] - sin_part[:, rows:]
    imag = cos_part[:, rows:] + sin_part[:, :rows]
    return real, imag


def combine_packed(products, out_len):
    swapped = pltpu.roll(products[out_len:], PACKED, 1)
    lane = lax.broadcasted_iota(jnp.int32, swapped.shape, 1)
    return products[:out_len] + jnp.where(lane < PACKED, -swapped, swapped)


def row_forward_kernel(core_ref, own_ref, other_ref, twist_ref, table_ref, *refs):
    *out_refs, part_ref = refs
    rows = own_ref.shape[1]
    width = part_ref.shape[2]
    per_half = RADIX // 2

    def small(step, _):
        row = pl.multiple_of(step * 8, 8)
        for lane in range(width // 128):
            lanes = pl.ds(lane * 128, 128)
            values = [
                half_ref[0, pl.ds(row, 8), pl.ds(index * width + lane * 128, 128)]
                for half_ref in (own_ref, other_ref)
                for index in range(per_half)
            ]
            for index, value in enumerate(small_real_fourier(values, -1)):
                real, imag = twist(value, twist_ref, index, lanes)
                part_ref[index, pl.ds(row, 8), lanes] = real
                part_ref[index, pl.ds(rows + row, 8), lanes] = imag
        return 0

    lax.fori_loop(0, rows // 8, small, 0)
    blocks, _, _, per_part, _ = out_refs[0].shape
    piece = per_part // RADIX
    per_block = piece * len(out_refs)

    def line(index, _):
        values = combine(matmul_split(table_ref, part_ref[index]), blocks * per_block, rows)
        for block in range(blocks):
            for part, out_ref in enumerate(out_refs):
                start = block * per_block + part * piece
                for side, value in enumerate(values):
                    out_ref[block, 0, side, pl.ds(index, piece, stride=RADIX), :] = value[
                        start : start + piece
                    ]
        return 0

    lax.fori_loop(0, RADIX, line, 0)


def complex_lines(read, rows, width, sign, twist_ref, part_ref):
    def small(step, _):
        row = pl.multiple_of(step * 8, 8)
        for lane in range(width // 128):
            lanes = pl.ds(lane * 128, 128)
            values = [
                (read(index, 0, pl.ds(row, 8), lanes), read(index, 1, pl.ds(row, 8), lanes))
                for index in range(RADIX)
            ]
            for index, value in enumerate(small_fourier(values, sign)):
                real, imag = twist(value, twist_ref, index, lanes)
                part_ref[index, pl.ds(row, 8), lanes] = real
                part_ref[index, pl.ds(rows + row, 8), lanes] = imag
        return 0

    lax.fori_loop(0, rows // 8, small, 0)


def column_forward_kernel(x_ref, twist_ref, table_ref, out_ref, part_ref, order_ref):
    rows = x_ref.shape[3]
    width = x_ref.shape[4]

    def read(index, part, row, lanes):
        return x_ref[index, 0, part, row, lanes]

    complex_lines(read, rows, width, -1, twist_ref, part_ref)

    def line(index, _):
        order_ref[pl.ds(index, width, stride=RADIX), :] = combine_packed(
            matmul_split(table_ref, part_ref[index]), width
        )
        return 0

    lax.fori_loop(0, RADIX, line, 0)

    def flip(index, _):
        start = pl.multiple_of(index * width, width)
        flipped = order_ref[pl.ds(start, width), :].T
        out_ref[0, 0, :, pl.ds(start, width)] = flipped[:rows]
        out_ref[0, 1, :, pl.ds(start, width)] = flipped[rows:]
        return 0

    lax.fori_loop(0, RADIX, flip, 0)


def column_inverse_kernel(
    counts, w0_ref, w1_ref, w2_ref, w3_ref, unmix_ref, twist_ref, table_ref, *refs
):
    *out_refs, mixed_ref, part_ref = refs
    component = pl.program_id(0)
    step = pl.program_id(1)
    rows = mixed_ref.shape[2]
    width = mixed_ref.shape[3]

    def mix(block, _):
        row = pl.multiple_of(block * 16, 16)
        for layer, wave in enumerate((w0_ref, w1_ref, w2_ref, w3_ref)):
            weight_real = unmix_ref[0, 0, layer, pl.ds(row, 16), :].astype(jnp.float32)
            weight_imag = unmix_ref[1, 0, layer, pl.ds(row, 16), :].astype(jnp.float32)
            wave_real = wave[0, 0, pl.ds(row, 16), :]
            wave_imag = wave[0, 1, pl.ds(row, 16), :]
            term_real = weight_real * wave_real - weight_imag * wave_imag
            term_imag = weight_real * wave_imag + weight_imag * wave_real
            real = term_real if layer == 0 else real + term_real
            imag = term_imag if layer == 0 else imag + term_imag
        mixed_ref[step, 0, pl.ds(row, 16), :] = real
        mixed_ref[step, 1, pl.ds(row, 16), :] = imag
        return 0

    lax.fori_loop(0, rows // 16, mix, 0)

    @pl.when(step == RADIX - 1)
    def _():
        def read(index, part, row, lanes):
            return mixed_ref[index, part, row, lanes]

        complex_lines(read, rows, width, 1, twist_ref, part_ref)
        blocks, _, per_block, _ = out_refs[0].shape
        piece = per_block // RADIX

        def lines(out_ref):
            def line(index, _):
                packed = combine_packed(matmul_split(table_ref, part_ref[index]), width)
                for block in range(blocks):
                    out_ref[block, 0, pl.ds(index, piece, stride=RADIX), :] = packed[
                        block * piece : (block + 1) * piece
                    ]
                return 0

            lax.fori_loop(0, RADIX, line, 0)

        first = 0
        for count, out_ref in zip(counts, out_refs):
            inside = (component >= first) & (component < first + count)
            pl.when(inside)(functools.partial(lines, out_ref))
            first += count


def row_inverse_kernel(core_ref, low_ref, high_ref, twist_ref, table_ref, *refs):
    out_ref, sent_ref, part_ref, order_ref = refs[-4:]
    rows = low_ref.shape[2]
    width = low_ref.shape[3]
    count = 2 * RADIX
    lanes = pl.ds(0, width)
    first_lanes = lax.broadcasted_iota(jnp.int32, (8, width), 1) < PACKED

    def small(step, _):
        row = pl.multiple_of(step * 8, 8)
        packed = [
            (low_ref[index, 0, pl.ds(row, 8), :], high_ref[index, 0, pl.ds(row, 8), :])
            for index in range(RADIX)
        ]
        whole_values = [
            (
                jnp.where(first_lanes, low, pltpu.roll(high, PACKED, 1)),
                jnp.where(first_lanes, pltpu.roll(low, PACKED, 1), high),
            )
            for low, high in packed
        ]
        for odd in range(2):
            values = whole_values
            if odd:
                values = [turn(value, index, count) for index, value in enumerate(values)]
            for index, value in enumerate(small_fourier(values, 1)):
                real, imag = twist(value, twist_ref, 2 * index + odd, lanes)
                part_ref[2 * index + odd, pl.ds(row, 8), pl.ds(0, width)] = real
                part_ref[2 * index + odd, pl.ds(row, 8), pl.ds(width, width)] = imag
        return 0

    lax.fori_loop(0, rows // 8, small, 0)
    out_len = table_ref.shape[1]

    def line(index, _):
        order_ref[pl.ds(index, out_len, stride=count), :] = matmul_split(table_ref, part_ref[index])
        return 0

    lax.fori_loop(0, count, line, 0)
    half_len = sent_ref.shape[2]
    chunk = 256
    own = core_ref[0] * half_len
    other = half_len - own

    def flip(index, _):
        start = pl.multiple_of(index * chunk, chunk)
        own_start = pl.multiple_of(own + start, chunk)
        other_start = pl.multiple_of(other + start, chunk)
        sent_ref[0, :, pl.ds(start, chunk)] = order_ref[pl.ds(other_start, chunk), :].T
        out_ref[0, :, pl.ds(start, chunk)] = order_ref[pl.ds(own_start, chunk), :].T
        return 0

    lax.fori_loop(0, half_len // chunk, flip, 0)


def whole(array):
    return pl.BlockSpec(array.shape, lambda *_: (0,) * array.ndim)


VMEM_LIMIT = 56 * 1024 * 1024
ROW_TILE = 128


def params(rank):
    return pltpu.CompilerParams(
        dimension_semantics=("arbitrary",) * rank, vmem_limit_bytes=VMEM_LIMIT
    )


def row_forward(layers, other, core, first, blocks, per_block, parts):
    count, rows, half_len = other.shape
    length = 2 * half_len
    width = length // RADIX
    tiles = rows // ROW_TILE
    per_part = per_block // parts
    signs = jnp.where(jnp.arange(RADIX) % 2 == 1, 1.0 - 2.0 * core[0].astype(jnp.float32), 1.0)
    twists = jnp.asarray(twiddle_table(RADIX, width, length, -1)) * signs[:, None, None, None]
    table = jnp.asarray(line_table(blocks * per_block // RADIX, width, -1))
    return pl.pallas_call(
        row_forward_kernel,
        grid_spec=pltpu.PrefetchScalarGridSpec(
            num_scalar_prefetch=1,
            grid=(count, tiles),
            in_specs=[
                pl.BlockSpec(
                    (1, ROW_TILE, half_len), lambda m, i, c: (first + m, c[0] * tiles + i, 0)
                ),
                pl.BlockSpec((1, ROW_TILE, half_len), lambda m, i, c: (m, i, 0)),
                whole(twists),
                whole(table),
            ],
            out_specs=[
                pl.BlockSpec((blocks, 1, 2, per_part, ROW_TILE), lambda m, i, c: (0, m, 0, 0, i))
            ]
            * parts,
            scratch_shapes=[pltpu.VMEM((RADIX, 2 * ROW_TILE, width), jnp.float32)],
        ),
        out_shape=[jax.ShapeDtypeStruct((blocks, count, 2, per_part, rows), jnp.float32)] * parts,
        compiler_params=params(2),
        name="row_forward",
    )(core, layers, other, twists, table)


def column_forward(x):
    blocks, count, _, rows, width = x.shape
    length = RADIX * width
    twists = jnp.asarray(twiddle_table(RADIX, width, length, -1))
    table = jnp.asarray(line_table(width, width, -1))
    return pl.pallas_call(
        column_forward_kernel,
        grid=(count, rows // PACKED),
        in_specs=[
            pl.BlockSpec((blocks, 1, 2, PACKED, width), lambda m, i: (0, m, 0, i, 0)),
            whole(twists),
            whole(table),
        ],
        out_specs=pl.BlockSpec((1, 2, PACKED, length), lambda m, i: (m, 0, i, 0)),
        out_shape=jax.ShapeDtypeStruct((count, 2, rows, length), jnp.float32),
        scratch_shapes=[
            pltpu.VMEM((RADIX, 2 * PACKED, width), jnp.float32),
            pltpu.VMEM((length, 2 * PACKED), jnp.float32),
        ],
        compiler_params=params(2),
        name="column_forward",
    )(x, twists, table)


def column_inverse(waves, unmixing, half, counts, blocks):
    length = waves[0][0].shape[3]
    width = length // RADIX
    per_block = length // blocks
    twists = jnp.asarray(twiddle_table(RADIX, width, length, 1))
    table = jnp.asarray(line_table(width, width, 1))

    def wave_spec(place, part):
        return pl.BlockSpec((1, 2, PACKED, width), lambda j, i: (place, 0, part, i))

    def out_spec(first, count):
        return pl.BlockSpec(
            (blocks, 1, per_block, 2 * PACKED),
            lambda j, i: (0, jnp.clip(j - first, 0, count - 1), 0, 0),
        )

    return pl.pallas_call(
        functools.partial(column_inverse_kernel, counts),
        grid=(sum(counts), RADIX),
        in_specs=[wave_spec(place, part) for _, place, part in waves]
        + [
            pl.BlockSpec((2, 1, len(waves), PACKED, width), lambda j, i: (0, j, 0, half, i)),
            whole(twists),
            whole(table),
        ],
        out_specs=[out_spec(sum(counts[:place]), count) for place, count in enumerate(counts)],
        out_shape=[
            jax.ShapeDtypeStruct((blocks, count, per_block, 2 * PACKED), jnp.float32)
            for count in counts
        ],
        scratch_shapes=[
            pltpu.VMEM((RADIX, 2, PACKED, width), jnp.float32),
            pltpu.VMEM((RADIX, 2 * PACKED, width), jnp.float32),
        ],
        compiler_params=params(2),
        name="column_inverse",
    )(*[wave for wave, _, _ in waves], unmixing, twists, table)


def row_inverse(low, high, first, group, shape, fields, core, scale):
    blocks, _, rows, width = low[0].shape
    half_len = shape[2]
    length = 2 * half_len
    count = 2 * RADIX
    tiles = rows // ROW_TILE
    twists = jnp.asarray(twiddle_table(count, width, length, 1))
    table = jnp.asarray(real_table(length // count, width, scale))
    held = [] if fields is None else [fields]

    def packed_spec(place):
        return pl.BlockSpec((blocks, 1, ROW_TILE, width), lambda m, i, c: (0, place + m, i, 0))

    return pl.pallas_call(
        row_inverse_kernel,
        grid_spec=pltpu.PrefetchScalarGridSpec(
            num_scalar_prefetch=1,
            grid=(group, tiles),
            in_specs=[packed_spec(low[1]), packed_spec(high[1]), whole(twists), whole(table)]
            + [pl.BlockSpec(memory_space=pl.ANY)] * len(held),
            out_specs=[
                pl.BlockSpec(
                    (1, ROW_TILE, half_len), lambda m, i, c: (first + m, c[0] * tiles + i, 0)
                ),
                pl.BlockSpec((1, ROW_TILE, half_len), lambda m, i, c: (m, i, 0)),
            ],
            scratch_shapes=[
                pltpu.VMEM((count, ROW_TILE, 2 * width), jnp.float32),
                pltpu.VMEM((length, ROW_TILE), jnp.float32),
            ],
        ),
        out_shape=[
            jax.ShapeDtypeStruct(shape, jnp.float32),
            jax.ShapeDtypeStruct((group, rows, half_len), jnp.float32),
        ],
        input_output_aliases={5: 0} if held else {},
        compiler_params=params(2),
        name="row_inverse",
    )(core, low[0], high[0], twists, table, *held)


def phase_pair(first_len, second_len, period, sign):
    first = lax.broadcasted_iota(jnp.int32, (first_len, second_len), 0)
    second = lax.broadcasted_iota(jnp.int32, (first_len, second_len), 1)
    turns = (first * second % period).astype(jnp.float32)
    phase = turns * (sign * 2.0 * math.pi / period)
    return (jnp.cos(phase), jnp.sin(phase))


def contract_first(values, table):
    return jnp.einsum("...qp,qk->...pk", values, table, precision=lax.Precision.HIGHEST)


def contract_second(values, table):
    return jnp.einsum("...pk,pj->...jk", values, table, precision=lax.Precision.HIGHEST)


def fourier(real_in, imag_in, length, sign, in_len, out_len, real_only):
    inner_len = min(length, 128)
    outer_len = length // inner_len
    rows_in = in_len // outer_len
    rows_out = out_len // inner_len
    leading = real_in.shape[:-1]
    first_cos, first_sin = phase_pair(rows_in, inner_len, inner_len, sign)
    first_table = jnp.concatenate([first_cos, first_sin], axis=1)
    both = contract_first(real_in.reshape(leading + (rows_in, outer_len)), first_table)
    part_real = both[..., :inner_len]
    part_imag = both[..., inner_len:]
    if imag_in is not None:
        other = contract_first(imag_in.reshape(leading + (rows_in, outer_len)), first_table)
        part_real = part_real - other[..., inner_len:]
        part_imag = part_imag + other[..., :inner_len]
    twist_cos, twist_sin = phase_pair(outer_len, inner_len, length, sign)
    turned_real = part_real * twist_cos - part_imag * twist_sin
    turned_imag = part_real * twist_sin + part_imag * twist_cos
    stacked = jnp.concatenate([turned_real, turned_imag], axis=-2)
    second_cos, second_sin = phase_pair(outer_len, rows_out, outer_len, sign)
    table_real = jnp.concatenate([second_cos, -second_sin], axis=0)
    if real_only:
        result_real = contract_second(stacked, table_real)
        return result_real.reshape(leading + (out_len,))
    table_imag = jnp.concatenate([second_sin, second_cos], axis=0)
    combined = contract_second(stacked, jnp.concatenate([table_real, table_imag], axis=1))
    result_real = combined[..., :rows_out, :].reshape(leading + (out_len,))
    result_imag = combined[..., rows_out:, :].reshape(leading + (out_len,))
    return (result_real, result_imag)


def reorder_blocks(values, row_count, col_count):
    leading = values.shape[0]
    block = values.shape[1] // (row_count * col_count)
    width = values.shape[2]
    split = values.reshape(leading, col_count, row_count, block, width)
    return jnp.transpose(split, (0, 4, 2, 1, 3)).reshape(
        leading, width, row_count * col_count * block
    )


def general_shards(layers, unmixing):
    row_count = lax.axis_size("row")
    col_count = lax.axis_size("col")
    rows_len = layers.shape[1] * row_count
    cols_len = layers.shape[2] * col_count
    spec_real, spec_imag = fourier(
        lax.all_to_all(layers, "col", split_axis=1, concat_axis=2, tiled=True),
        None,
        cols_len,
        -1.0,
        cols_len,
        cols_len // 2,
        False,
    )
    moved_real, moved_imag = (
        lax.all_to_all(
            lax.all_to_all(spec_real, "row", split_axis=2, concat_axis=1, tiled=True),
            "col",
            split_axis=2,
            concat_axis=1,
            tiled=True,
        ),
        lax.all_to_all(
            lax.all_to_all(spec_imag, "row", split_axis=2, concat_axis=1, tiled=True),
            "col",
            split_axis=2,
            concat_axis=1,
            tiled=True,
        ),
    )
    line_real = reorder_blocks(moved_real, row_count, col_count)
    line_imag = reorder_blocks(moved_imag, row_count, col_count)
    wave_real, wave_imag = fourier(line_real, line_imag, rows_len, -1.0, rows_len, rows_len, False)
    mixed_real = None
    mixed_imag = None
    for layer_index in range(4):
        weight_real = unmixing[0, :, layer_index].astype(jnp.float32)
        weight_imag = unmixing[1, :, layer_index].astype(jnp.float32)
        layer_real = wave_real[layer_index][None]
        layer_imag = wave_imag[layer_index][None]
        term_real = weight_real * layer_real - weight_imag * layer_imag
        term_imag = weight_real * layer_imag + weight_imag * layer_real
        if mixed_real is None:
            mixed_real = term_real
            mixed_imag = term_imag
        else:
            mixed_real = mixed_real + term_real
            mixed_imag = mixed_imag + term_imag
    back_real, back_imag = fourier(mixed_real, mixed_imag, rows_len, 1.0, rows_len, rows_len, False)
    scale = 2.0 / (rows_len * cols_len)
    sent_real, sent_imag = (
        lax.all_to_all(
            lax.all_to_all(back_real, "row", split_axis=2, concat_axis=1, tiled=True),
            "col",
            split_axis=2,
            concat_axis=1,
            tiled=True,
        ),
        lax.all_to_all(
            lax.all_to_all(back_imag, "row", split_axis=2, concat_axis=1, tiled=True),
            "col",
            split_axis=2,
            concat_axis=1,
            tiled=True,
        ),
    )
    grid_real = reorder_blocks(sent_real, row_count, col_count)
    grid_imag = reorder_blocks(sent_imag, row_count, col_count)
    fields = fourier(grid_real, grid_imag, cols_len, 1.0, cols_len // 2, cols_len, True)
    fields = fields * scale
    return lax.all_to_all(fields, "col", split_axis=2, concat_axis=1, tiled=True)


def swap_cores(values):
    return lax.ppermute(values, "col", [(0, 1), (1, 0)])


def exchange_all(ready):
    moved = []
    for values in ready:
        if moved:
            values, moved[-1] = lax.optimization_barrier((values, moved[-1]))
        moved.append(
            lax.all_to_all(values, ("row", "col"), split_axis=0, concat_axis=0, tiled=True)
        )
    return moved


def layer_shards(layers, unmixing):
    row_count = lax.axis_size("row")
    col_count = lax.axis_size("col")
    blocks = row_count * col_count
    layer_count, block_rows, half_len = layers.shape
    rows = block_rows // col_count
    per_block = unmixing.shape[3]
    core = lax.axis_index("col").astype(jnp.int32).reshape(1)
    other_row = rows - core[0] * rows

    def lines(source, first, count, parts):
        given = lax.dynamic_slice(source, (first, other_row, 0), (count, rows, half_len))
        other = swap_cores(given)
        return row_forward(layers, other, core, first, blocks, per_block, parts)

    (head,) = lines(layers, 0, 1, 1)
    source, head = lax.optimization_barrier((layers, head))
    rest = lines(source, 1, layer_count - 1, 2)
    first_moved, *rest_moved = exchange_all([head, *rest])
    first_wave = column_forward(first_moved)
    waves = []
    for half, moved in enumerate(rest_moved):
        rest_waves = column_forward(moved)
        waves.append(
            [(first_wave, 0, half)] + [(rest_waves, place, 0) for place in range(layer_count - 1)]
        )
    early = unmixing.shape[1] - 1
    low, low_last = column_inverse(waves[0], unmixing, 0, (early, 1), blocks)
    high, high_last = column_inverse(waves[1], unmixing, 1, (early, 1), blocks)
    low, *_ = lax.optimization_barrier((low, rest_moved[-1]))
    last = jnp.concatenate([low_last, high_last], axis=1)
    low, high, last = exchange_all([low, high, last])
    scale = 2.0 / (block_rows * row_count * half_len * col_count)
    fields = None
    for first, group, low_part, high_part in (
        (0, early, (low, 0), (high, 0)),
        (early, 1, (last, 0), (last, 1)),
    ):
        fields, given = row_inverse(
            low_part, high_part, first, group, layers.shape, fields, core, scale
        )
        fields = lax.dynamic_update_slice(fields, swap_cores(given), (first, other_row, 0))
    return fields


def shards(layers, unmixing):
    col_count = lax.axis_size("col")
    blocks = lax.axis_size("row") * col_count
    shape = (blocks, col_count) + layers.shape + unmixing.shape[1:]
    if shape == (RADIX, 2, 4, 512, 2048, 4, 4, 128, 4096):
        return layer_shards(layers, unmixing)
    return general_shards(layers, unmixing)


def solution(mesh):
    in_specs = (P("tiles", "row", "col"), P("tiles", None, None, ("row", "col"), None))
    out_specs = P("tiles", "row", "col")
    return jax.shard_map(shards, mesh=mesh, in_specs=in_specs, out_specs=out_specs, check_vma=False)
```

```python
import functools
import math

import jax
import jax.numpy as jnp
import ml_dtypes
import numpy as np
from jax import lax
from jax.experimental import pallas as pl
from jax.experimental.pallas import tpu as pltpu
from jax.sharding import PartitionSpec as P

RADIX = 16
PACKED = 64


def split_table(table):
    high = table.astype(ml_dtypes.bfloat16)
    low = (table - high.astype(np.float64)).astype(ml_dtypes.bfloat16)
    return np.stack([high, low])


def twiddle_table(count, width, length, sign):
    turns = np.outer(np.arange(count), np.arange(width)) % length
    phase = turns * (sign * 2.0 * math.pi / length)
    pair = np.stack([np.cos(phase), np.sin(phase)], axis=1)
    return np.ascontiguousarray(
        np.broadcast_to(pair[:, :, None, :], (count, 2, 8, width))
    ).astype(np.float32)


def line_table(out_len, width, sign):
    turns = np.outer(np.arange(out_len), np.arange(width)) % width
    phase = turns * (sign * 2.0 * math.pi / width)
    return split_table(np.concatenate([np.cos(phase), np.sin(phase)], axis=0))


def real_table(out_len, width, scale):
    turns = np.outer(np.arange(out_len), np.arange(width)) % width
    phase = turns * (2.0 * math.pi / width)
    return split_table(scale * np.concatenate([np.cos(phase), -np.sin(phase)], axis=1))


def turn(value, numerator, denominator):
    real, imag = value
    numerator %= denominator
    eighths = 8 * numerator / denominator
    if eighths == 0:
        return (real, imag)
    if eighths == 2:
        return (-imag, real)
    if eighths == 4:
        return (-real, -imag)
    if eighths == 6:
        return (imag, -real)
    cos = math.cos(2.0 * math.pi * numerator / denominator)
    sin = math.sin(2.0 * math.pi * numerator / denominator)
    if eighths in (1, 3, 5, 7):
        half = math.sqrt(0.5)
        scaled_sum = (real + imag) * half
        scaled_gap = (real - imag) * half
        if eighths == 1:
            return (scaled_gap, scaled_sum)
        if eighths == 3:
            return (-scaled_sum, scaled_gap)
        if eighths == 5:
            return (-scaled_gap, -scaled_sum)
        return (scaled_sum, -scaled_gap)
    return (real * cos - imag * sin, real * sin + imag * cos)


def add(left, right):
    return (left[0] + right[0], left[1] + right[1])


def gap(left, right):
    return (left[0] - right[0], left[1] - right[1])


def small_fourier(values, sign):
    count = len(values)
    if count == 1:
        return values
    even = small_fourier(values[0::2], sign)
    odd = small_fourier(values[1::2], sign)
    odd = [turn(value, sign * index, count) for index, value in enumerate(odd)]
    return [add(e, o) for e, o in zip(even, odd)] + [gap(e, o) for e, o in zip(even, odd)]


def small_real_fourier(values, sign):
    count = len(values)
    if count == 2:
        zero = jnp.zeros_like(values[0])
        return [(values[0] + values[1], zero), (values[0] - values[1], zero)]
    even = small_real_fourier(values[0::2], sign)
    odd = small_real_fourier(values[1::2], sign)
    result = [None] * count
    for index in range(count // 4 + 1):
        turned = turn(odd[index], sign * index, count)
        upper = add(even[index], turned)
        lower = gap(even[index], turned)
        result[index] = upper
        result[count // 2 - index] = (lower[0], -lower[1])
    for index in range(1, count // 2):
        result[count - index] = (result[index][0], -result[index][1])
    return result


def twist(value, table_ref, index, lanes):
    if index == 0:
        return value
    cos = table_ref[index, 0, :, lanes]
    sin = table_ref[index, 1, :, lanes]
    return (value[0] * cos - value[1] * sin, value[0] * sin + value[1] * cos)


def dot_rows(table, values):
    return lax.dot_general(
        table, values, (((1,), (1,)), ((), ())), preferred_element_type=jnp.float32
    )


def matmul_split(table_ref, values):
    high = values.astype(jnp.bfloat16)
    low = (values - high.astype(jnp.float32)).astype(jnp.bfloat16)
    return (
        dot_rows(table_ref[0], high)
        + dot_rows(table_ref[0], low)
        + dot_rows(table_ref[1], high)
    )


def combine(products, out_len, rows):
    cos_part = products[:out_len]
    sin_part = products[out_len:]
    real = cos_part[:, :rows] - sin_part[:, rows:]
    imag = cos_part[:, rows:] + sin_part[:, :rows]
    return real, imag


def combine_packed(products, out_len):
    swapped = pltpu.roll(products[out_len:], PACKED, 1)
    lane = lax.broadcasted_iota(jnp.int32, swapped.shape, 1)
    return products[:out_len] + jnp.where(lane < PACKED, -swapped, swapped)


def row_forward_kernel(core_ref, own_ref, other_ref, twist_ref, table_ref, *refs):
    *out_refs, part_ref = refs
    rows = own_ref.shape[1]
    width = part_ref.shape[2]
    per_half = RADIX // 2

    def small(step, _):
        row = pl.multiple_of(step * 8, 8)
        for lane in range(width // 128):
            lanes = pl.ds(lane * 128, 128)
            values = [
                half_ref[0, pl.ds(row, 8), pl.ds(index * width + lane * 128, 128)]
                for half_ref in (own_ref, other_ref)
                for index in range(per_half)
            ]
            for index, value in enumerate(small_real_fourier(values, -1)):
                real, imag = twist(value, twist_ref, index, lanes)
                part_ref[index, pl.ds(row, 8), lanes] = real
                part_ref[index, pl.ds(rows + row, 8), lanes] = imag
        return 0

    lax.fori_loop(0, rows // 8, small, 0)
    blocks, _, _, per_part, _ = out_refs[0].shape
    piece = per_part // RADIX
    per_block = piece * len(out_refs)

    def line(index, _):
        values = combine(matmul_split(table_ref, part_ref[index]), blocks * per_block, rows)
        for block in range(blocks):
            for part, out_ref in enumerate(out_refs):
                start = block * per_block + part * piece
                for side, value in enumerate(values):
                    out_ref[block, 0, side, pl.ds(index, piece, stride=RADIX), :] = value[
                        start : start + piece
                    ]
        return 0

    lax.fori_loop(0, RADIX, line, 0, unroll=2)


def complex_lines(read, rows, width, sign, twist_ref, part_ref):
    def small(step, _):
        row = pl.multiple_of(step * 8, 8)
        for lane in range(width // 128):
            lanes = pl.ds(lane * 128, 128)
            values = [
                (read(index, 0, pl.ds(row, 8), lanes), read(index, 1, pl.ds(row, 8), lanes))
                for index in range(RADIX)
            ]
            for index, value in enumerate(small_fourier(values, sign)):
                real, imag = twist(value, twist_ref, index, lanes)
                part_ref[index, pl.ds(row, 8), lanes] = real
                part_ref[index, pl.ds(rows + row, 8), lanes] = imag
        return 0

    lax.fori_loop(0, rows // 8, small, 0)


def column_forward_kernel(x_ref, twist_ref, table_ref, out_ref, part_ref, order_ref):
    rows = x_ref.shape[3]
    width = x_ref.shape[4]

    def read(index, part, row, lanes):
        return x_ref[index, 0, part, row, lanes]

    complex_lines(read, rows, width, -1, twist_ref, part_ref)

    def line(index, _):
        order_ref[pl.ds(index, width, stride=RADIX), :] = combine_packed(
            matmul_split(table_ref, part_ref[index]), width
        )
        return 0

    lax.fori_loop(0, RADIX, line, 0, unroll=2)

    def flip(index, _):
        start = pl.multiple_of(index * width, width)
        flipped = order_ref[pl.ds(start, width), :].T
        out_ref[0, 0, :, pl.ds(start, width)] = flipped[:rows]
        out_ref[0, 1, :, pl.ds(start, width)] = flipped[rows:]
        return 0

    lax.fori_loop(0, RADIX, flip, 0)


def column_inverse_kernel(
    counts, w0_ref, w1_ref, w2_ref, w3_ref, unmix_ref, twist_ref, table_ref, *refs
):
    *out_refs, mixed_ref, part_ref = refs
    component = pl.program_id(0)
    step = pl.program_id(1)
    rows = mixed_ref.shape[2]
    width = mixed_ref.shape[3]

    def mix(block, _):
        row = pl.multiple_of(block * 16, 16)
        for layer, wave in enumerate((w0_ref, w1_ref, w2_ref, w3_ref)):
            weight_real = unmix_ref[0, 0, layer, pl.ds(row, 16), :].astype(jnp.float32)
            weight_imag = unmix_ref[1, 0, layer, pl.ds(row, 16), :].astype(jnp.float32)
            wave_real = wave[0, 0, pl.ds(row, 16), :]
            wave_imag = wave[0, 1, pl.ds(row, 16), :]
            term_real = weight_real * wave_real - weight_imag * wave_imag
            term_imag = weight_real * wave_imag + weight_imag * wave_real
            real = term_real if layer == 0 else real + term_real
            imag = term_imag if layer == 0 else imag + term_imag
        mixed_ref[step, 0, pl.ds(row, 16), :] = real
        mixed_ref[step, 1, pl.ds(row, 16), :] = imag
        return 0

    lax.fori_loop(0, rows // 16, mix, 0)

    @pl.when(step == RADIX - 1)
    def _():
        def read(index, part, row, lanes):
            return mixed_ref[index, part, row, lanes]

        complex_lines(read, rows, width, 1, twist_ref, part_ref)
        blocks, _, per_block, _ = out_refs[0].shape
        piece = per_block // RADIX

        def lines(out_ref):
            def line(index, _):
                packed = combine_packed(matmul_split(table_ref, part_ref[index]), width)
                for block in range(blocks):
                    out_ref[block, 0, pl.ds(index, piece, stride=RADIX), :] = packed[
                        block * piece : (block + 1) * piece
                    ]
                return 0

            lax.fori_loop(0, RADIX, line, 0, unroll=2)

        first = 0
        for count, out_ref in zip(counts, out_refs):
            inside = (component >= first) & (component < first + count)
            pl.when(inside)(functools.partial(lines, out_ref))
            first += count


def row_inverse_kernel(core_ref, low_ref, high_ref, twist_ref, table_ref, *refs):
    out_ref, sent_ref, part_ref, order_ref = refs[-4:]
    rows = low_ref.shape[2]
    width = low_ref.shape[3]
    count = 2 * RADIX
    lanes = pl.ds(0, width)
    first_lanes = lax.broadcasted_iota(jnp.int32, (8, width), 1) < PACKED

    def small(step, _):
        row = pl.multiple_of(step * 8, 8)
        packed = [
            (low_ref[index, 0, pl.ds(row, 8), :], high_ref[index, 0, pl.ds(row, 8), :])
            for index in range(RADIX)
        ]
        whole_values = [
            (
                jnp.where(first_lanes, low, pltpu.roll(high, PACKED, 1)),
                jnp.where(first_lanes, pltpu.roll(low, PACKED, 1), high),
            )
            for low, high in packed
        ]
        for odd in range(2):
            values = whole_values
            if odd:
                values = [turn(value, index, count) for index, value in enumerate(values)]
            for index, value in enumerate(small_fourier(values, 1)):
                real, imag = twist(value, twist_ref, 2 * index + odd, lanes)
                part_ref[2 * index + odd, pl.ds(row, 8), pl.ds(0, width)] = real
                part_ref[2 * index + odd, pl.ds(row, 8), pl.ds(width, width)] = imag
        return 0

    lax.fori_loop(0, rows // 8, small, 0)
    out_len = table_ref.shape[1]

    def line(index, _):
        order_ref[pl.ds(index, out_len, stride=count), :] = matmul_split(table_ref, part_ref[index])
        return 0

    lax.fori_loop(0, count, line, 0, unroll=4)
    half_len = sent_ref.shape[2]
    chunk = 256
    own = core_ref[0] * half_len
    other = half_len - own

    def flip(index, _):
        start = pl.multiple_of(index * chunk, chunk)
        own_start = pl.multiple_of(own + start, chunk)
        other_start = pl.multiple_of(other + start, chunk)
        sent_ref[0, :, pl.ds(start, chunk)] = order_ref[pl.ds(other_start, chunk), :].T
        out_ref[0, :, pl.ds(start, chunk)] = order_ref[pl.ds(own_start, chunk), :].T
        return 0

    lax.fori_loop(0, half_len // chunk, flip, 0)


def whole(array):
    return pl.BlockSpec(array.shape, lambda *_: (0,) * array.ndim)


VMEM_LIMIT = 56 * 1024 * 1024
ROW_TILE = 128


def params(rank):
    return pltpu.CompilerParams(
        dimension_semantics=("arbitrary",) * rank, vmem_limit_bytes=VMEM_LIMIT
    )


def row_forward(layers, other, core, first, blocks, per_block, parts):
    count, rows, half_len = other.shape
    length = 2 * half_len
    width = length // RADIX
    tiles = rows // ROW_TILE
    per_part = per_block // parts
    signs = jnp.where(jnp.arange(RADIX) % 2 == 1, 1.0 - 2.0 * core[0].astype(jnp.float32), 1.0)
    twists = jnp.asarray(twiddle_table(RADIX, width, length, -1)) * signs[:, None, None, None]
    table = jnp.asarray(line_table(blocks * per_block // RADIX, width, -1))
    return pl.pallas_call(
        row_forward_kernel,
        grid_spec=pltpu.PrefetchScalarGridSpec(
            num_scalar_prefetch=1,
            grid=(count, tiles),
            in_specs=[
                pl.BlockSpec(
                    (1, ROW_TILE, half_len), lambda m, i, c: (first + m, c[0] * tiles + i, 0)
                ),
                pl.BlockSpec((1, ROW_TILE, half_len), lambda m, i, c: (m, i, 0)),
                whole(twists),
                whole(table),
            ],
            out_specs=[
                pl.BlockSpec((blocks, 1, 2, per_part, ROW_TILE), lambda m, i, c: (0, m, 0, 0, i))
            ]
            * parts,
            scratch_shapes=[pltpu.VMEM((RADIX, 2 * ROW_TILE, width), jnp.float32)],
        ),
        out_shape=[jax.ShapeDtypeStruct((blocks, count, 2, per_part, rows), jnp.float32)] * parts,
        compiler_params=params(2),
        name="row_forward",
    )(core, layers, other, twists, table)


def column_forward(x):
    blocks, count, _, rows, width = x.shape
    length = RADIX * width
    twists = jnp.asarray(twiddle_table(RADIX, width, length, -1))
    table = jnp.asarray(line_table(width, width, -1))
    return pl.pallas_call(
        column_forward_kernel,
        grid=(count, rows // PACKED),
        in_specs=[
            pl.BlockSpec((blocks, 1, 2, PACKED, width), lambda m, i: (0, m, 0, i, 0)),
            whole(twists),
            whole(table),
        ],
        out_specs=pl.BlockSpec((1, 2, PACKED, length), lambda m, i: (m, 0, i, 0)),
        out_shape=jax.ShapeDtypeStruct((count, 2, rows, length), jnp.float32),
        scratch_shapes=[
            pltpu.VMEM((RADIX, 2 * PACKED, width), jnp.float32),
            pltpu.VMEM((length, 2 * PACKED), jnp.float32),
        ],
        compiler_params=params(2),
        name="column_forward",
    )(x, twists, table)


def column_inverse(waves, unmixing, half, counts, blocks):
    length = waves[0][0].shape[3]
    width = length // RADIX
    per_block = length // blocks
    twists = jnp.asarray(twiddle_table(RADIX, width, length, 1))
    table = jnp.asarray(line_table(width, width, 1))

    def wave_spec(place, part):
        return pl.BlockSpec((1, 2, PACKED, width), lambda j, i: (place, 0, part, i))

    def out_spec(first, count):
        return pl.BlockSpec(
            (blocks, 1, per_block, 2 * PACKED),
            lambda j, i: (0, jnp.clip(j - first, 0, count - 1), 0, 0),
        )

    return pl.pallas_call(
        functools.partial(column_inverse_kernel, counts),
        grid=(sum(counts), RADIX),
        in_specs=[wave_spec(place, part) for _, place, part in waves]
        + [
            pl.BlockSpec((2, 1, len(waves), PACKED, width), lambda j, i: (0, j, 0, half, i)),
            whole(twists),
            whole(table),
        ],
        out_specs=[out_spec(sum(counts[:place]), count) for place, count in enumerate(counts)],
        out_shape=[
            jax.ShapeDtypeStruct((blocks, count, per_block, 2 * PACKED), jnp.float32)
            for count in counts
        ],
        scratch_shapes=[
            pltpu.VMEM((RADIX, 2, PACKED, width), jnp.float32),
            pltpu.VMEM((RADIX, 2 * PACKED, width), jnp.float32),
        ],
        compiler_params=params(2),
        name="column_inverse",
    )(*[wave for wave, _, _ in waves], unmixing, twists, table)


def row_inverse(low, high, first, group, shape, fields, core, scale):
    blocks, _, rows, width = low[0].shape
    half_len = shape[2]
    length = 2 * half_len
    count = 2 * RADIX
    tiles = rows // ROW_TILE
    twists = jnp.asarray(twiddle_table(count, width, length, 1))
    table = jnp.asarray(real_table(length // count, width, scale))
    held = [] if fields is None else [fields]

    def packed_spec(place):
        return pl.BlockSpec((blocks, 1, ROW_TILE, width), lambda m, i, c: (0, place + m, i, 0))

    return pl.pallas_call(
        row_inverse_kernel,
        grid_spec=pltpu.PrefetchScalarGridSpec(
            num_scalar_prefetch=1,
            grid=(group, tiles),
            in_specs=[packed_spec(low[1]), packed_spec(high[1]), whole(twists), whole(table)]
            + [pl.BlockSpec(memory_space=pl.ANY)] * len(held),
            out_specs=[
                pl.BlockSpec(
                    (1, ROW_TILE, half_len), lambda m, i, c: (first + m, c[0] * tiles + i, 0)
                ),
                pl.BlockSpec((1, ROW_TILE, half_len), lambda m, i, c: (m, i, 0)),
            ],
            scratch_shapes=[
                pltpu.VMEM((count, ROW_TILE, 2 * width), jnp.float32),
                pltpu.VMEM((length, ROW_TILE), jnp.float32),
            ],
        ),
        out_shape=[
            jax.ShapeDtypeStruct(shape, jnp.float32),
            jax.ShapeDtypeStruct((group, rows, half_len), jnp.float32),
        ],
        input_output_aliases={5: 0} if held else {},
        compiler_params=params(2),
        name="row_inverse",
    )(core, low[0], high[0], twists, table, *held)


def phase_pair(first_len, second_len, period, sign):
    first = lax.broadcasted_iota(jnp.int32, (first_len, second_len), 0)
    second = lax.broadcasted_iota(jnp.int32, (first_len, second_len), 1)
    turns = (first * second % period).astype(jnp.float32)
    phase = turns * (sign * 2.0 * math.pi / period)
    return (jnp.cos(phase), jnp.sin(phase))


def contract_first(values, table):
    return jnp.einsum("...qp,qk->...pk", values, table, precision=lax.Precision.HIGHEST)


def contract_second(values, table):
    return jnp.einsum("...pk,pj->...jk", values, table, precision=lax.Precision.HIGHEST)


def fourier(real_in, imag_in, length, sign, in_len, out_len, real_only):
    inner_len = min(length, 128)
    outer_len = length // inner_len
    rows_in = in_len // outer_len
    rows_out = out_len // inner_len
    leading = real_in.shape[:-1]
    first_cos, first_sin = phase_pair(rows_in, inner_len, inner_len, sign)
    first_table = jnp.concatenate([first_cos, first_sin], axis=1)
    both = contract_first(real_in.reshape(leading + (rows_in, outer_len)), first_table)
    part_real = both[..., :inner_len]
    part_imag = both[..., inner_len:]
    if imag_in is not None:
        other = contract_first(imag_in.reshape(leading + (rows_in, outer_len)), first_table)
        part_real = part_real - other[..., inner_len:]
        part_imag = part_imag + other[..., :inner_len]
    twist_cos, twist_sin = phase_pair(outer_len, inner_len, length, sign)
    turned_real = part_real * twist_cos - part_imag * twist_sin
    turned_imag = part_real * twist_sin + part_imag * twist_cos
    stacked = jnp.concatenate([turned_real, turned_imag], axis=-2)
    second_cos, second_sin = phase_pair(outer_len, rows_out, outer_len, sign)
    table_real = jnp.concatenate([second_cos, -second_sin], axis=0)
    if real_only:
        result_real = contract_second(stacked, table_real)
        return result_real.reshape(leading + (out_len,))
    table_imag = jnp.concatenate([second_sin, second_cos], axis=0)
    combined = contract_second(stacked, jnp.concatenate([table_real, table_imag], axis=1))
    result_real = combined[..., :rows_out, :].reshape(leading + (out_len,))
    result_imag = combined[..., rows_out:, :].reshape(leading + (out_len,))
    return (result_real, result_imag)


def reorder_blocks(values, row_count, col_count):
    leading = values.shape[0]
    block = values.shape[1] // (row_count * col_count)
    width = values.shape[2]
    split = values.reshape(leading, col_count, row_count, block, width)
    return jnp.transpose(split, (0, 4, 2, 1, 3)).reshape(
        leading, width, row_count * col_count * block
    )


def general_shards(layers, unmixing):
    row_count = lax.axis_size("row")
    col_count = lax.axis_size("col")
    rows_len = layers.shape[1] * row_count
    cols_len = layers.shape[2] * col_count
    spec_real, spec_imag = fourier(
        lax.all_to_all(layers, "col", split_axis=1, concat_axis=2, tiled=True),
        None,
        cols_len,
        -1.0,
        cols_len,
        cols_len // 2,
        False,
    )
    moved_real, moved_imag = (
        lax.all_to_all(
            lax.all_to_all(spec_real, "row", split_axis=2, concat_axis=1, tiled=True),
            "col",
            split_axis=2,
            concat_axis=1,
            tiled=True,
        ),
        lax.all_to_all(
            lax.all_to_all(spec_imag, "row", split_axis=2, concat_axis=1, tiled=True),
            "col",
            split_axis=2,
            concat_axis=1,
            tiled=True,
        ),
    )
    line_real = reorder_blocks(moved_real, row_count, col_count)
    line_imag = reorder_blocks(moved_imag, row_count, col_count)
    wave_real, wave_imag = fourier(line_real, line_imag, rows_len, -1.0, rows_len, rows_len, False)
    mixed_real = None
    mixed_imag = None
    for layer_index in range(4):
        weight_real = unmixing[0, :, layer_index].astype(jnp.float32)
        weight_imag = unmixing[1, :, layer_index].astype(jnp.float32)
        layer_real = wave_real[layer_index][None]
        layer_imag = wave_imag[layer_index][None]
        term_real = weight_real * layer_real - weight_imag * layer_imag
        term_imag = weight_real * layer_imag + weight_imag * layer_real
        if mixed_real is None:
            mixed_real = term_real
            mixed_imag = term_imag
        else:
            mixed_real = mixed_real + term_real
            mixed_imag = mixed_imag + term_imag
    back_real, back_imag = fourier(mixed_real, mixed_imag, rows_len, 1.0, rows_len, rows_len, False)
    scale = 2.0 / (rows_len * cols_len)
    sent_real, sent_imag = (
        lax.all_to_all(
            lax.all_to_all(back_real, "row", split_axis=2, concat_axis=1, tiled=True),
            "col",
            split_axis=2,
            concat_axis=1,
            tiled=True,
        ),
        lax.all_to_all(
            lax.all_to_all(back_imag, "row", split_axis=2, concat_axis=1, tiled=True),
            "col",
            split_axis=2,
            concat_axis=1,
            tiled=True,
        ),
    )
    grid_real = reorder_blocks(sent_real, row_count, col_count)
    grid_imag = reorder_blocks(sent_imag, row_count, col_count)
    fields = fourier(grid_real, grid_imag, cols_len, 1.0, cols_len // 2, cols_len, True)
    fields = fields * scale
    return lax.all_to_all(fields, "col", split_axis=2, concat_axis=1, tiled=True)


def swap_cores(values):
    return lax.ppermute(values, "col", [(0, 1), (1, 0)])


def exchange_all(ready):
    moved = []
    for values in ready:
        if moved:
            values, moved[-1] = lax.optimization_barrier((values, moved[-1]))
        moved.append(
            lax.all_to_all(values, ("row", "col"), split_axis=0, concat_axis=0, tiled=True)
        )
    return moved


def layer_shards(layers, unmixing):
    row_count = lax.axis_size("row")
    col_count = lax.axis_size("col")
    blocks = row_count * col_count
    layer_count, block_rows, half_len = layers.shape
    rows = block_rows // col_count
    per_block = unmixing.shape[3]
    core = lax.axis_index("col").astype(jnp.int32).reshape(1)
    other_row = rows - core[0] * rows

    def lines(source, first, count, parts):
        given = lax.dynamic_slice(source, (first, other_row, 0), (count, rows, half_len))
        other = swap_cores(given)
        return row_forward(layers, other, core, first, blocks, per_block, parts)

    (head,) = lines(layers, 0, 1, 1)
    source, head = lax.optimization_barrier((layers, head))
    rest = lines(source, 1, layer_count - 1, 2)
    first_moved, *rest_moved = exchange_all([head, *rest])
    first_wave = column_forward(first_moved)
    waves = []
    for half, moved in enumerate(rest_moved):
        rest_waves = column_forward(moved)
        waves.append(
            [(first_wave, 0, half)] + [(rest_waves, place, 0) for place in range(layer_count - 1)]
        )
    early = unmixing.shape[1] - 1
    low, low_last = column_inverse(waves[0], unmixing, 0, (early, 1), blocks)
    high, high_last = column_inverse(waves[1], unmixing, 1, (early, 1), blocks)
    low, *_ = lax.optimization_barrier((low, rest_moved[-1]))
    last = jnp.concatenate([low_last, high_last], axis=1)
    low, high, last = exchange_all([low, high, last])
    scale = 2.0 / (block_rows * row_count * half_len * col_count)
    fields = None
    for first, group, low_part, high_part in (
        (0, early, (low, 0), (high, 0)),
        (early, 1, (last, 0), (last, 1)),
    ):
        fields, given = row_inverse(
            low_part, high_part, first, group, layers.shape, fields, core, scale
        )
        fields = lax.dynamic_update_slice(fields, swap_cores(given), (first, other_row, 0))
    return fields


def shards(layers, unmixing):
    col_count = lax.axis_size("col")
    blocks = lax.axis_size("row") * col_count
    shape = (blocks, col_count) + layers.shape + unmixing.shape[1:]
    if shape == (RADIX, 2, 4, 512, 2048, 4, 4, 128, 4096):
        return layer_shards(layers, unmixing)
    return general_shards(layers, unmixing)


def solution(mesh):
    in_specs = (P("tiles", "row", "col"), P("tiles", None, None, ("row", "col"), None))
    out_specs = P("tiles", "row", "col")
    return jax.shard_map(shards, mesh=mesh, in_specs=in_specs, out_specs=out_specs, check_vma=False)
```

```python
import functools
import math

import jax
import jax.numpy as jnp
import ml_dtypes
import numpy as np
from jax import lax
from jax.experimental import pallas as pl
from jax.experimental.pallas import tpu as pltpu
from jax.sharding import PartitionSpec as P

RADIX = 16
PACKED = 64


def split_table(table):
    high = table.astype(ml_dtypes.bfloat16)
    low = (table - high.astype(np.float64)).astype(ml_dtypes.bfloat16)
    return np.stack([high, low])


def twiddle_table(count, width, length, sign):
    turns = np.outer(np.arange(count), np.arange(width)) % length
    phase = turns * (sign * 2.0 * math.pi / length)
    pair = np.stack([np.cos(phase), np.sin(phase)], axis=1)
    return np.ascontiguousarray(
        np.broadcast_to(pair[:, :, None, :], (count, 2, 8, width))
    ).astype(np.float32)


def line_table(out_len, width, sign):
    turns = np.outer(np.arange(out_len), np.arange(width)) % width
    phase = turns * (sign * 2.0 * math.pi / width)
    return split_table(np.concatenate([np.cos(phase), np.sin(phase)], axis=0))


def real_table(out_len, width, scale):
    turns = np.outer(np.arange(out_len), np.arange(width)) % width
    phase = turns * (2.0 * math.pi / width)
    return split_table(scale * np.concatenate([np.cos(phase), -np.sin(phase)], axis=1))


def turn(value, numerator, denominator):
    real, imag = value
    numerator %= denominator
    eighths = 8 * numerator / denominator
    if eighths == 0:
        return (real, imag)
    if eighths == 2:
        return (-imag, real)
    if eighths == 4:
        return (-real, -imag)
    if eighths == 6:
        return (imag, -real)
    cos = math.cos(2.0 * math.pi * numerator / denominator)
    sin = math.sin(2.0 * math.pi * numerator / denominator)
    if eighths in (1, 3, 5, 7):
        half = math.sqrt(0.5)
        scaled_sum = (real + imag) * half
        scaled_gap = (real - imag) * half
        if eighths == 1:
            return (scaled_gap, scaled_sum)
        if eighths == 3:
            return (-scaled_sum, scaled_gap)
        if eighths == 5:
            return (-scaled_gap, -scaled_sum)
        return (scaled_sum, -scaled_gap)
    return (real * cos - imag * sin, real * sin + imag * cos)


def add(left, right):
    return (left[0] + right[0], left[1] + right[1])


def gap(left, right):
    return (left[0] - right[0], left[1] - right[1])


def small_fourier(values, sign):
    count = len(values)
    if count == 1:
        return values
    even = small_fourier(values[0::2], sign)
    odd = small_fourier(values[1::2], sign)
    odd = [turn(value, sign * index, count) for index, value in enumerate(odd)]
    return [add(e, o) for e, o in zip(even, odd)] + [gap(e, o) for e, o in zip(even, odd)]


def small_real_fourier(values, sign):
    count = len(values)
    if count == 2:
        zero = jnp.zeros_like(values[0])
        return [(values[0] + values[1], zero), (values[0] - values[1], zero)]
    even = small_real_fourier(values[0::2], sign)
    odd = small_real_fourier(values[1::2], sign)
    result = [None] * count
    for index in range(count // 4 + 1):
        turned = turn(odd[index], sign * index, count)
        upper = add(even[index], turned)
        lower = gap(even[index], turned)
        result[index] = upper
        result[count // 2 - index] = (lower[0], -lower[1])
    for index in range(1, count // 2):
        result[count - index] = (result[index][0], -result[index][1])
    return result


def twist(value, table_ref, index, lanes):
    if index == 0:
        return value
    cos = table_ref[index, 0, :, lanes]
    sin = table_ref[index, 1, :, lanes]
    return (value[0] * cos - value[1] * sin, value[0] * sin + value[1] * cos)


def dot_rows(table, values):
    return lax.dot_general(
        table, values, (((1,), (1,)), ((), ())), preferred_element_type=jnp.float32
    )


def matmul_split(table_ref, values):
    high = values.astype(jnp.bfloat16)
    low = (values - high.astype(jnp.float32)).astype(jnp.bfloat16)
    return (
        dot_rows(table_ref[0], high)
        + dot_rows(table_ref[0], low)
        + dot_rows(table_ref[1], high)
    )


def combine(products, out_len, rows):
    cos_part = products[:out_len]
    sin_part = products[out_len:]
    real = cos_part[:, :rows] - sin_part[:, rows:]
    imag = cos_part[:, rows:] + sin_part[:, :rows]
    return real, imag


def combine_packed(products, out_len):
    swapped = pltpu.roll(products[out_len:], PACKED, 1)
    lane = lax.broadcasted_iota(jnp.int32, swapped.shape, 1)
    return products[:out_len] + jnp.where(lane < PACKED, -swapped, swapped)


def row_forward_kernel(core_ref, own_ref, other_ref, twist_ref, table_ref, *refs):
    *out_refs, part_ref = refs
    rows = own_ref.shape[1]
    width = part_ref.shape[2]
    per_half = RADIX // 2

    def small(step, _):
        row = pl.multiple_of(step * 8, 8)
        for lane in range(width // 128):
            lanes = pl.ds(lane * 128, 128)
            values = [
                half_ref[0, pl.ds(row, 8), pl.ds(index * width + lane * 128, 128)]
                for half_ref in (own_ref, other_ref)
                for index in range(per_half)
            ]
            for index, value in enumerate(small_real_fourier(values, -1)):
                real, imag = twist(value, twist_ref, index, lanes)
                part_ref[index, pl.ds(row, 8), lanes] = real
                part_ref[index, pl.ds(rows + row, 8), lanes] = imag
        return 0

    lax.fori_loop(0, rows // 8, small, 0)
    blocks, _, _, per_part, _ = out_refs[0].shape
    piece = per_part // RADIX
    per_block = piece * len(out_refs)

    def line(index, _):
        values = combine(matmul_split(table_ref, part_ref[index]), blocks * per_block, rows)
        for block in range(blocks):
            for part, out_ref in enumerate(out_refs):
                start = block * per_block + part * piece
                for side, value in enumerate(values):
                    out_ref[block, 0, side, pl.ds(index, piece, stride=RADIX), :] = value[
                        start : start + piece
                    ]
        return 0

    lax.fori_loop(0, RADIX, line, 0, unroll=4)


def complex_lines(read, rows, width, sign, twist_ref, part_ref):
    def small(step, _):
        row = pl.multiple_of(step * 8, 8)
        for lane in range(width // 128):
            lanes = pl.ds(lane * 128, 128)
            values = [
                (read(index, 0, pl.ds(row, 8), lanes), read(index, 1, pl.ds(row, 8), lanes))
                for index in range(RADIX)
            ]
            for index, value in enumerate(small_fourier(values, sign)):
                real, imag = twist(value, twist_ref, index, lanes)
                part_ref[index, pl.ds(row, 8), lanes] = real
                part_ref[index, pl.ds(rows + row, 8), lanes] = imag
        return 0

    lax.fori_loop(0, rows // 8, small, 0)


def column_forward_kernel(x_ref, twist_ref, table_ref, out_ref, part_ref, order_ref):
    rows = x_ref.shape[3]
    width = x_ref.shape[4]

    def read(index, part, row, lanes):
        return x_ref[index, 0, part, row, lanes]

    complex_lines(read, rows, width, -1, twist_ref, part_ref)

    def line(index, _):
        order_ref[pl.ds(index, width, stride=RADIX), :] = combine_packed(
            matmul_split(table_ref, part_ref[index]), width
        )
        return 0

    lax.fori_loop(0, RADIX, line, 0, unroll=2)

    def flip(index, _):
        start = pl.multiple_of(index * width, width)
        flipped = order_ref[pl.ds(start, width), :].T
        out_ref[0, 0, :, pl.ds(start, width)] = flipped[:rows]
        out_ref[0, 1, :, pl.ds(start, width)] = flipped[rows:]
        return 0

    lax.fori_loop(0, RADIX, flip, 0)


def column_inverse_kernel(
    counts, w0_ref, w1_ref, w2_ref, w3_ref, unmix_ref, twist_ref, table_ref, *refs
):
    *out_refs, mixed_ref, part_ref = refs
    component = pl.program_id(0)
    step = pl.program_id(1)
    rows = mixed_ref.shape[2]
    width = mixed_ref.shape[3]

    def mix(block, _):
        row = pl.multiple_of(block * 16, 16)
        for layer, wave in enumerate((w0_ref, w1_ref, w2_ref, w3_ref)):
            weight_real = unmix_ref[0, 0, layer, pl.ds(row, 16), :].astype(jnp.float32)
            weight_imag = unmix_ref[1, 0, layer, pl.ds(row, 16), :].astype(jnp.float32)
            wave_real = wave[0, 0, pl.ds(row, 16), :]
            wave_imag = wave[0, 1, pl.ds(row, 16), :]
            term_real = weight_real * wave_real - weight_imag * wave_imag
            term_imag = weight_real * wave_imag + weight_imag * wave_real
            real = term_real if layer == 0 else real + term_real
            imag = term_imag if layer == 0 else imag + term_imag
        mixed_ref[step, 0, pl.ds(row, 16), :] = real
        mixed_ref[step, 1, pl.ds(row, 16), :] = imag
        return 0

    lax.fori_loop(0, rows // 16, mix, 0)

    @pl.when(step == RADIX - 1)
    def _():
        def read(index, part, row, lanes):
            return mixed_ref[index, part, row, lanes]

        complex_lines(read, rows, width, 1, twist_ref, part_ref)
        blocks, _, per_block, _ = out_refs[0].shape
        piece = per_block // RADIX

        def lines(out_ref):
            def line(index, _):
                packed = combine_packed(matmul_split(table_ref, part_ref[index]), width)
                for block in range(blocks):
                    out_ref[block, 0, pl.ds(index, piece, stride=RADIX), :] = packed[
                        block * piece : (block + 1) * piece
                    ]
                return 0

            lax.fori_loop(0, RADIX, line, 0, unroll=2)

        first = 0
        for count, out_ref in zip(counts, out_refs):
            inside = (component >= first) & (component < first + count)
            pl.when(inside)(functools.partial(lines, out_ref))
            first += count


def row_inverse_kernel(core_ref, low_ref, high_ref, twist_ref, table_ref, *refs):
    out_ref, sent_ref, part_ref, order_ref = refs[-4:]
    rows = low_ref.shape[2]
    width = low_ref.shape[3]
    count = 2 * RADIX
    lanes = pl.ds(0, width)
    first_lanes = lax.broadcasted_iota(jnp.int32, (8, width), 1) < PACKED

    def small(step, _):
        row = pl.multiple_of(step * 8, 8)
        packed = [
            (low_ref[index, 0, pl.ds(row, 8), :], high_ref[index, 0, pl.ds(row, 8), :])
            for index in range(RADIX)
        ]
        whole_values = [
            (
                jnp.where(first_lanes, low, pltpu.roll(high, PACKED, 1)),
                jnp.where(first_lanes, pltpu.roll(low, PACKED, 1), high),
            )
            for low, high in packed
        ]
        for odd in range(2):
            values = whole_values
            if odd:
                values = [turn(value, index, count) for index, value in enumerate(values)]
            for index, value in enumerate(small_fourier(values, 1)):
                real, imag = twist(value, twist_ref, 2 * index + odd, lanes)
                part_ref[2 * index + odd, pl.ds(row, 8), pl.ds(0, width)] = real
                part_ref[2 * index + odd, pl.ds(row, 8), pl.ds(width, width)] = imag
        return 0

    lax.fori_loop(0, rows // 8, small, 0)
    out_len = table_ref.shape[1]

    def line(index, _):
        order_ref[pl.ds(index, out_len, stride=count), :] = matmul_split(table_ref, part_ref[index])
        return 0

    lax.fori_loop(0, count, line, 0, unroll=4)
    half_len = sent_ref.shape[2]
    chunk = 256
    own = core_ref[0] * half_len
    other = half_len - own

    def flip(index, _):
        start = pl.multiple_of(index * chunk, chunk)
        own_start = pl.multiple_of(own + start, chunk)
        other_start = pl.multiple_of(other + start, chunk)
        sent_ref[0, :, pl.ds(start, chunk)] = order_ref[pl.ds(other_start, chunk), :].T
        out_ref[0, :, pl.ds(start, chunk)] = order_ref[pl.ds(own_start, chunk), :].T
        return 0

    lax.fori_loop(0, half_len // chunk, flip, 0)


def whole(array):
    return pl.BlockSpec(array.shape, lambda *_: (0,) * array.ndim)


VMEM_LIMIT = 56 * 1024 * 1024
ROW_TILE = 128


def params(rank):
    return pltpu.CompilerParams(
        dimension_semantics=("arbitrary",) * rank, vmem_limit_bytes=VMEM_LIMIT
    )


def row_forward(layers, other, core, first, blocks, per_block, parts):
    count, rows, half_len = other.shape
    length = 2 * half_len
    width = length // RADIX
    tiles = rows // ROW_TILE
    per_part = per_block // parts
    signs = jnp.where(jnp.arange(RADIX) % 2 == 1, 1.0 - 2.0 * core[0].astype(jnp.float32), 1.0)
    twists = jnp.asarray(twiddle_table(RADIX, width, length, -1)) * signs[:, None, None, None]
    table = jnp.asarray(line_table(blocks * per_block // RADIX, width, -1))
    return pl.pallas_call(
        row_forward_kernel,
        grid_spec=pltpu.PrefetchScalarGridSpec(
            num_scalar_prefetch=1,
            grid=(count, tiles),
            in_specs=[
                pl.BlockSpec(
                    (1, ROW_TILE, half_len), lambda m, i, c: (first + m, c[0] * tiles + i, 0)
                ),
                pl.BlockSpec((1, ROW_TILE, half_len), lambda m, i, c: (m, i, 0)),
                whole(twists),
                whole(table),
            ],
            out_specs=[
                pl.BlockSpec((blocks, 1, 2, per_part, ROW_TILE), lambda m, i, c: (0, m, 0, 0, i))
            ]
            * parts,
            scratch_shapes=[pltpu.VMEM((RADIX, 2 * ROW_TILE, width), jnp.float32)],
        ),
        out_shape=[jax.ShapeDtypeStruct((blocks, count, 2, per_part, rows), jnp.float32)] * parts,
        compiler_params=params(2),
        name="row_forward",
    )(core, layers, other, twists, table)


def column_forward(x):
    blocks, count, _, rows, width = x.shape
    length = RADIX * width
    twists = jnp.asarray(twiddle_table(RADIX, width, length, -1))
    table = jnp.asarray(line_table(width, width, -1))
    return pl.pallas_call(
        column_forward_kernel,
        grid=(count, rows // PACKED),
        in_specs=[
            pl.BlockSpec((blocks, 1, 2, PACKED, width), lambda m, i: (0, m, 0, i, 0)),
            whole(twists),
            whole(table),
        ],
        out_specs=pl.BlockSpec((1, 2, PACKED, length), lambda m, i: (m, 0, i, 0)),
        out_shape=jax.ShapeDtypeStruct((count, 2, rows, length), jnp.float32),
        scratch_shapes=[
            pltpu.VMEM((RADIX, 2 * PACKED, width), jnp.float32),
            pltpu.VMEM((length, 2 * PACKED), jnp.float32),
        ],
        compiler_params=params(2),
        name="column_forward",
    )(x, twists, table)


def column_inverse(waves, unmixing, half, counts, blocks):
    length = waves[0][0].shape[3]
    width = length // RADIX
    per_block = length // blocks
    twists = jnp.asarray(twiddle_table(RADIX, width, length, 1))
    table = jnp.asarray(line_table(width, width, 1))

    def wave_spec(place, part):
        return pl.BlockSpec((1, 2, PACKED, width), lambda j, i: (place, 0, part, i))

    def out_spec(first, count):
        return pl.BlockSpec(
            (blocks, 1, per_block, 2 * PACKED),
            lambda j, i: (0, jnp.clip(j - first, 0, count - 1), 0, 0),
        )

    return pl.pallas_call(
        functools.partial(column_inverse_kernel, counts),
        grid=(sum(counts), RADIX),
        in_specs=[wave_spec(place, part) for _, place, part in waves]
        + [
            pl.BlockSpec((2, 1, len(waves), PACKED, width), lambda j, i: (0, j, 0, half, i)),
            whole(twists),
            whole(table),
        ],
        out_specs=[out_spec(sum(counts[:place]), count) for place, count in enumerate(counts)],
        out_shape=[
            jax.ShapeDtypeStruct((blocks, count, per_block, 2 * PACKED), jnp.float32)
            for count in counts
        ],
        scratch_shapes=[
            pltpu.VMEM((RADIX, 2, PACKED, width), jnp.float32),
            pltpu.VMEM((RADIX, 2 * PACKED, width), jnp.float32),
        ],
        compiler_params=params(2),
        name="column_inverse",
    )(*[wave for wave, _, _ in waves], unmixing, twists, table)


def row_inverse(low, high, first, group, shape, fields, core, scale):
    blocks, _, rows, width = low[0].shape
    half_len = shape[2]
    length = 2 * half_len
    count = 2 * RADIX
    tiles = rows // ROW_TILE
    twists = jnp.asarray(twiddle_table(count, width, length, 1))
    table = jnp.asarray(real_table(length // count, width, scale))
    held = [] if fields is None else [fields]

    def packed_spec(place):
        return pl.BlockSpec((blocks, 1, ROW_TILE, width), lambda m, i, c: (0, place + m, i, 0))

    return pl.pallas_call(
        row_inverse_kernel,
        grid_spec=pltpu.PrefetchScalarGridSpec(
            num_scalar_prefetch=1,
            grid=(group, tiles),
            in_specs=[packed_spec(low[1]), packed_spec(high[1]), whole(twists), whole(table)]
            + [pl.BlockSpec(memory_space=pl.ANY)] * len(held),
            out_specs=[
                pl.BlockSpec(
                    (1, ROW_TILE, half_len), lambda m, i, c: (first + m, c[0] * tiles + i, 0)
                ),
                pl.BlockSpec((1, ROW_TILE, half_len), lambda m, i, c: (m, i, 0)),
            ],
            scratch_shapes=[
                pltpu.VMEM((count, ROW_TILE, 2 * width), jnp.float32),
                pltpu.VMEM((length, ROW_TILE), jnp.float32),
            ],
        ),
        out_shape=[
            jax.ShapeDtypeStruct(shape, jnp.float32),
            jax.ShapeDtypeStruct((group, rows, half_len), jnp.float32),
        ],
        input_output_aliases={5: 0} if held else {},
        compiler_params=params(2),
        name="row_inverse",
    )(core, low[0], high[0], twists, table, *held)


def phase_pair(first_len, second_len, period, sign):
    first = lax.broadcasted_iota(jnp.int32, (first_len, second_len), 0)
    second = lax.broadcasted_iota(jnp.int32, (first_len, second_len), 1)
    turns = (first * second % period).astype(jnp.float32)
    phase = turns * (sign * 2.0 * math.pi / period)
    return (jnp.cos(phase), jnp.sin(phase))


def contract_first(values, table):
    return jnp.einsum("...qp,qk->...pk", values, table, precision=lax.Precision.HIGHEST)


def contract_second(values, table):
    return jnp.einsum("...pk,pj->...jk", values, table, precision=lax.Precision.HIGHEST)


def fourier(real_in, imag_in, length, sign, in_len, out_len, real_only):
    inner_len = min(length, 128)
    outer_len = length // inner_len
    rows_in = in_len // outer_len
    rows_out = out_len // inner_len
    leading = real_in.shape[:-1]
    first_cos, first_sin = phase_pair(rows_in, inner_len, inner_len, sign)
    first_table = jnp.concatenate([first_cos, first_sin], axis=1)
    both = contract_first(real_in.reshape(leading + (rows_in, outer_len)), first_table)
    part_real = both[..., :inner_len]
    part_imag = both[..., inner_len:]
    if imag_in is not None:
        other = contract_first(imag_in.reshape(leading + (rows_in, outer_len)), first_table)
        part_real = part_real - other[..., inner_len:]
        part_imag = part_imag + other[..., :inner_len]
    twist_cos, twist_sin = phase_pair(outer_len, inner_len, length, sign)
    turned_real = part_real * twist_cos - part_imag * twist_sin
    turned_imag = part_real * twist_sin + part_imag * twist_cos
    stacked = jnp.concatenate([turned_real, turned_imag], axis=-2)
    second_cos, second_sin = phase_pair(outer_len, rows_out, outer_len, sign)
    table_real = jnp.concatenate([second_cos, -second_sin], axis=0)
    if real_only:
        result_real = contract_second(stacked, table_real)
        return result_real.reshape(leading + (out_len,))
    table_imag = jnp.concatenate([second_sin, second_cos], axis=0)
    combined = contract_second(stacked, jnp.concatenate([table_real, table_imag], axis=1))
    result_real = combined[..., :rows_out, :].reshape(leading + (out_len,))
    result_imag = combined[..., rows_out:, :].reshape(leading + (out_len,))
    return (result_real, result_imag)


def reorder_blocks(values, row_count, col_count):
    leading = values.shape[0]
    block = values.shape[1] // (row_count * col_count)
    width = values.shape[2]
    split = values.reshape(leading, col_count, row_count, block, width)
    return jnp.transpose(split, (0, 4, 2, 1, 3)).reshape(
        leading, width, row_count * col_count * block
    )


def general_shards(layers, unmixing):
    row_count = lax.axis_size("row")
    col_count = lax.axis_size("col")
    rows_len = layers.shape[1] * row_count
    cols_len = layers.shape[2] * col_count
    spec_real, spec_imag = fourier(
        lax.all_to_all(layers, "col", split_axis=1, concat_axis=2, tiled=True),
        None,
        cols_len,
        -1.0,
        cols_len,
        cols_len // 2,
        False,
    )
    moved_real, moved_imag = (
        lax.all_to_all(
            lax.all_to_all(spec_real, "row", split_axis=2, concat_axis=1, tiled=True),
            "col",
            split_axis=2,
            concat_axis=1,
            tiled=True,
        ),
        lax.all_to_all(
            lax.all_to_all(spec_imag, "row", split_axis=2, concat_axis=1, tiled=True),
            "col",
            split_axis=2,
            concat_axis=1,
            tiled=True,
        ),
    )
    line_real = reorder_blocks(moved_real, row_count, col_count)
    line_imag = reorder_blocks(moved_imag, row_count, col_count)
    wave_real, wave_imag = fourier(line_real, line_imag, rows_len, -1.0, rows_len, rows_len, False)
    mixed_real = None
    mixed_imag = None
    for layer_index in range(4):
        weight_real = unmixing[0, :, layer_index].astype(jnp.float32)
        weight_imag = unmixing[1, :, layer_index].astype(jnp.float32)
        layer_real = wave_real[layer_index][None]
        layer_imag = wave_imag[layer_index][None]
        term_real = weight_real * layer_real - weight_imag * layer_imag
        term_imag = weight_real * layer_imag + weight_imag * layer_real
        if mixed_real is None:
            mixed_real = term_real
            mixed_imag = term_imag
        else:
            mixed_real = mixed_real + term_real
            mixed_imag = mixed_imag + term_imag
    back_real, back_imag = fourier(mixed_real, mixed_imag, rows_len, 1.0, rows_len, rows_len, False)
    scale = 2.0 / (rows_len * cols_len)
    sent_real, sent_imag = (
        lax.all_to_all(
            lax.all_to_all(back_real, "row", split_axis=2, concat_axis=1, tiled=True),
            "col",
            split_axis=2,
            concat_axis=1,
            tiled=True,
        ),
        lax.all_to_all(
            lax.all_to_all(back_imag, "row", split_axis=2, concat_axis=1, tiled=True),
            "col",
            split_axis=2,
            concat_axis=1,
            tiled=True,
        ),
    )
    grid_real = reorder_blocks(sent_real, row_count, col_count)
    grid_imag = reorder_blocks(sent_imag, row_count, col_count)
    fields = fourier(grid_real, grid_imag, cols_len, 1.0, cols_len // 2, cols_len, True)
    fields = fields * scale
    return lax.all_to_all(fields, "col", split_axis=2, concat_axis=1, tiled=True)


def swap_cores(values):
    return lax.ppermute(values, "col", [(0, 1), (1, 0)])


def exchange_all(ready):
    moved = []
    for values in ready:
        if moved:
            values, moved[-1] = lax.optimization_barrier((values, moved[-1]))
        moved.append(
            lax.all_to_all(values, ("row", "col"), split_axis=0, concat_axis=0, tiled=True)
        )
    return moved


def layer_shards(layers, unmixing):
    row_count = lax.axis_size("row")
    col_count = lax.axis_size("col")
    blocks = row_count * col_count
    layer_count, block_rows, half_len = layers.shape
    rows = block_rows // col_count
    per_block = unmixing.shape[3]
    core = lax.axis_index("col").astype(jnp.int32).reshape(1)
    other_row = rows - core[0] * rows

    def lines(source, first, count, parts):
        given = lax.dynamic_slice(source, (first, other_row, 0), (count, rows, half_len))
        other = swap_cores(given)
        return row_forward(layers, other, core, first, blocks, per_block, parts)

    (head,) = lines(layers, 0, 1, 1)
    source, head = lax.optimization_barrier((layers, head))
    rest = lines(source, 1, layer_count - 1, 2)
    first_moved, *rest_moved = exchange_all([head, *rest])
    first_wave = column_forward(first_moved)
    waves = []
    for half, moved in enumerate(rest_moved):
        rest_waves = column_forward(moved)
        waves.append(
            [(first_wave, 0, half)] + [(rest_waves, place, 0) for place in range(layer_count - 1)]
        )
    early = unmixing.shape[1] - 1
    low, low_last = column_inverse(waves[0], unmixing, 0, (early, 1), blocks)
    high, high_last = column_inverse(waves[1], unmixing, 1, (early, 1), blocks)
    low, *_ = lax.optimization_barrier((low, rest_moved[-1]))
    last = jnp.concatenate([low_last, high_last], axis=1)
    low, high, last = exchange_all([low, high, last])
    scale = 2.0 / (block_rows * row_count * half_len * col_count)
    fields = None
    for first, group, low_part, high_part in (
        (0, early, (low, 0), (high, 0)),
        (early, 1, (last, 0), (last, 1)),
    ):
        fields, given = row_inverse(
            low_part, high_part, first, group, layers.shape, fields, core, scale
        )
        fields = lax.dynamic_update_slice(fields, swap_cores(given), (first, other_row, 0))
    return fields


def shards(layers, unmixing):
    col_count = lax.axis_size("col")
    blocks = lax.axis_size("row") * col_count
    shape = (blocks, col_count) + layers.shape + unmixing.shape[1:]
    if shape == (RADIX, 2, 4, 512, 2048, 4, 4, 128, 4096):
        return layer_shards(layers, unmixing)
    return general_shards(layers, unmixing)


def solution(mesh):
    in_specs = (P("tiles", "row", "col"), P("tiles", None, None, ("row", "col"), None))
    out_specs = P("tiles", "row", "col")
    return jax.shard_map(shards, mesh=mesh, in_specs=in_specs, out_specs=out_specs, check_vma=False)
```
